256 devices in a mesh: rep: 2 (over z_hi), zero: 128 (over z_lo, y, x, core).
Axes of the slice: x: 4, y: 4, z: 8 (z_hi: 2, z_lo: 4; z = z_hi * 4 + z_lo), core: 2. Of those that a mesh axis runs over, the one named last changes fastest.
Arguments:
- acts: bfloat16 [256, 8192], P('rep', 'zero'), may hold values from -6 to 6
- grads_out: bfloat16 [256, 8192], P('rep', 'zero'), may hold values from -12 to 12
- act_inverse: bfloat16 [8192, 8192], P('zero'), as said below
- grad_inverse: bfloat16 [8192, 8192], P('zero'), as said below
Outputs:
- precond: float32 [8192, 8192], P('zero')
The draws below stay inside these ranges and needn't reach their ends.
Inputs may be any that keep to these rules, and one draw needn't show every extreme that they name: act_inverse is symmetric. grad_inverse is symmetric.
All inputs are finite; a program needn't handle non-finite values.
Results may differ from the reference program's by a relative error of at most 0.004.
Values may be sent and summed in bfloat16 or wider, within the bound.
No kernel may reach another device: no remote copies, remote signals or barrier semaphores. Data moves between devices by JAX's collectives and lax.ppermute only.
A program may use at most 64 MiB of HBM per device.

```python
import math
import jax
import jax.numpy as jnp
from jax import lax

D = 8192
TOKENS = 256


def make_inverse(key):
    key_raw, key_diag = jax.random.split(key, 2)
    raw = jax.random.normal(key_raw, (D, D), jnp.float32) / math.sqrt(D)
    matrix = (raw + raw.T) * 0.5
    diagonal = jax.random.uniform(key_diag, (D,), jnp.float32, 1.5, 3.0)
    matrix = matrix + jnp.diag(diagonal)
    return matrix.astype(jnp.bfloat16)


def draw_act_inverse(key, part):
    return make_inverse(jax.random.fold_in(key, 11))


def draw_grad_inverse(key, part):
    return make_inverse(jax.random.fold_in(key, 23))


def shard_levels(key, dims, shards, smallest, largest):
    loudness = 1.0
    for dim, shards_of in shards:
        draws = jax.random.uniform(jax.random.fold_in(jax.random.fold_in(key, 6), dim), (shards_of,), jnp.float32, smallest / len(shards), largest / len(shards))
        loudness = loudness * jnp.repeat(jnp.exp(draws), dims[dim] // shards_of).reshape((-1,) + (1,) * (len(dims) - 1 - dim))
    return loudness


def scatter_about(stream_key, shape, scale, bound, cuts=(), held_as=jnp.bfloat16):
    gain = shard_levels(stream_key, shape, cuts, -0.22, 0.18) if cuts else 1.0
    entries = jax.random.normal(stream_key, shape, jnp.float32) * scale * gain
    return jnp.minimum(jnp.maximum(entries, -bound), bound).astype(held_as)


def setup_inputs(seed: int = 0) -> dict:
    splits = jax.random.split(jax.random.key(seed), 5)
    acts = scatter_about(splits[0], (TOKENS, D), 1.0, 6.0, ((0, 2), (1, 128)))
    grads_out = scatter_about(splits[1], (TOKENS, D), 2.0, 12.0, ((0, 2), (1, 128)))
    act_inverse = draw_act_inverse(jax.random.fold_in(splits[4], 71), 0)
    grad_inverse = draw_grad_inverse(jax.random.fold_in(splits[4], 71), 0)
    return {"acts": acts, "grads_out": grads_out, "act_inverse": act_inverse, "grad_inverse": grad_inverse}


def reference(acts, grads_out, act_inverse, grad_inverse):
    act_pre = jnp.dot(acts, act_inverse, preferred_element_type=jnp.float32).astype(jnp.bfloat16)
    grad_pre = jnp.dot(grads_out, grad_inverse, preferred_element_type=jnp.float32).astype(jnp.bfloat16)
    summed = lax.dot_general(grad_pre, act_pre, (((0,), (0,)), ((), ())), preferred_element_type=jnp.float32)
    return summed / jnp.float32(TOKENS)
```

```python
import functools

import jax
import jax.numpy as jnp
from jax import lax
from jax.experimental import pallas as pl
from jax.experimental.pallas import tpu as pltpu
from jax.sharding import Mesh
from jax.sharding import PartitionSpec as P

AXES = ("rep", "zl", "y", "x", "c")
SIZES = (2, 4, 4, 4, 2)
ZERO = AXES[1:]
TOKENS = 256


def places():
    for r in range(2):
        for zl in range(4):
            for y in range(4):
                for x in range(4):
                    for c in range(2):
                        yield r, zl, y, x, c


def rank(r, zl, y, x, c):
    return (((r * 4 + zl % 4) * 4 + y % 4) * 4 + x % 4) * 2 + c


def send(value, target):
    pairs = [(rank(*place), rank(*target(*place))) for place in places()]
    return lax.ppermute(value, AXES, pairs)


def swap_cores(value):
    return send(value, lambda r, zl, y, x, c: (r, zl, y, x, 1 - c))


def along_line(value, k):
    return send(value, lambda r, zl, y, x, c: (r, zl + k, y, x, c))


def along_ring(value, k):
    return send(
        value,
        lambda r, zl, y, x, c: ((r * 4 + zl + k) // 4 % 2, zl + k, y, x, c),
    )


def first_turn(value, k):
    return send(
        value,
        lambda r, zl, y, x, c: (r, zl, y, x + k, c) if c else (r, zl, y + k, x, c),
    )


def second_turn(value, k):
    return send(
        value,
        lambda r, zl, y, x, c: (r, zl, y + k, x, c) if c else (r, zl, y, x + k, c),
    )


def block_of(where, core, k3, k2, kz):
    zl = lax.rem(where[0] + 4 - kz, 4)
    k_y = jnp.where(core == 0, k2, k3)
    k_x = jnp.where(core == 0, k3, k2)
    y = lax.rem(where[1] + 4 - k_y, 4)
    x = lax.rem(where[2] + 4 - k_x, 4)
    return pl.multiple_of(((zl * 4 + y) * 4 + x) * 128, 128)


def precondition(where, p0, p1, p2, p3, mine, theirs, pre):
    core = where[3]
    total = jnp.zeros((128, 128), jnp.float32)
    for k3, piece in enumerate((p0, p1, p2, p3)):
        for k2 in range(4):
            rows, cols = [], []
            for kz in range(4):
                at = block_of(where, core, k3, k2, kz)
                cols.append(piece[k2, kz])
                rows.append(
                    jnp.concatenate(
                        [mine[:, pl.ds(at, 128)], theirs[:, pl.ds(at, 128)]], axis=0
                    )
                )
            total += lax.dot_general(
                jnp.concatenate(cols, axis=1),
                jnp.concatenate(rows, axis=1),
                (((1,), (1,)), ((), ())),
                preferred_element_type=jnp.float32,
            )
    swapped = pltpu.roll(total, 64, 1)
    pre[...] = jnp.where(core == 0, total, swapped).astype(pre.dtype)


def outer(zs, where, g_own, g_other, *refs):
    pieces, out = refs[:-1], refs[-1]
    core = where[3]
    for side, grads in enumerate((g_own, g_other)):
        left = grads[...]
        held_by = core if side == 0 else 1 - core
        for k3 in range(4):
            piece = pieces[side * 4 + k3]
            for k2 in range(4):
                wide = jnp.concatenate([piece[k2, j] for j in range(4)], axis=1)
                part = lax.dot_general(
                    left,
                    wide,
                    (((1,), (0,)), ((), ())),
                    preferred_element_type=jnp.float32,
                ) * (1.0 / TOKENS)
                for j, kz in enumerate(zs):
                    at = block_of(where, held_by, k3, k2, kz)
                    block = part[:, j * 128 : (j + 1) * 128]
                    if side == 0:
                        out[:, pl.ds(at, 128)] = block
                    else:
                        out[:, pl.ds(at, 128)] += block


VMEM = pl.BlockSpec(memory_space=pltpu.VMEM)
SMEM = pl.BlockSpec(memory_space=pltpu.SMEM)
PARAMS = pltpu.CompilerParams(vmem_limit_bytes=40 * 1024 * 1024)


def on_device(acts, grads_out, act_inverse, grad_inverse):
    r, c = lax.axis_index("rep"), lax.axis_index("c")
    where = jnp.stack(
        [lax.axis_index("zl"), lax.axis_index("y"), lax.axis_index("x"), c]
    ).astype(jnp.int32)
    first = c == 0

    got = swap_cores(jnp.where(first, grads_out, acts))
    kept = jnp.where(first, acts, grads_out)
    block = jnp.concatenate(
        [jnp.where(first, kept, got), jnp.where(first, got, kept)], axis=1
    )
    theirs = swap_cores(jnp.where(first, grad_inverse, act_inverse))
    mine = jnp.where(first, act_inverse, grad_inverse)

    line = jnp.stack([block] + [along_line(block, k) for k in (1, 2, 3)])
    plane = jnp.stack([line] + [first_turn(line, k) for k in (1, 2, 3)])
    pieces = [plane] + [second_turn(plane, k) for k in (1, 2, 3)]
    pre = pl.pallas_call(
        precondition,
        out_shape=jax.ShapeDtypeStruct((128, 128), jnp.bfloat16),
        in_specs=[SMEM] + [VMEM] * 6,
        out_specs=VMEM,
        compiler_params=PARAMS,
        name="precondition",
    )(where, *pieces, mine, theirs)

    far = send(
        pre, lambda r, zl, y, x, c: (1 - r, zl, y, x, 1 - r if c else r)
    )
    near = swap_cores(pre)
    block = jnp.where(r != c, far, jnp.where(first, pre, near))
    passed = swap_cores(far)
    g_here = jnp.where(first, near, pre)
    g_there = jnp.where(r == c, far, passed)
    own_tokens = r == c
    g_own = jnp.where(own_tokens, g_here, g_there)
    g_other = jnp.where(own_tokens, g_there, g_here)
    g_own, g_other = (
        jnp.where(first, g[:, :64], g[:, 64:]).T for g in (g_own, g_other)
    )

    line = jnp.stack([block] + [along_ring(block, k) for k in (1, 7, 2)])
    plane = jnp.stack([line] + [first_turn(line, k) for k in (1, 2, 3)])
    pieces = [plane] + [second_turn(plane, k) for k in (1, 2, 3)]
    others = [swap_cores(piece) for piece in pieces]
    return pl.pallas_call(
        functools.partial(outer, (0, 1, 3, 2)),
        out_shape=jax.ShapeDtypeStruct((64, 8192), jnp.float32),
        in_specs=[SMEM] + [VMEM] * 10,
        out_specs=VMEM,
        compiler_params=PARAMS,
        name="outer",
    )(where, g_own, g_other, *pieces, *others)


def solution(mesh):
    finer = Mesh(mesh.devices.reshape(SIZES), AXES)
    return jax.shard_map(
        on_device,
        mesh=finer,
        in_specs=(P("rep", ZERO), P("rep", ZERO), P(ZERO, None), P(ZERO, None)),
        out_specs=P(ZERO, None),
        check_vma=False,
    )
```

```python
import jax
import jax.numpy as jnp
from jax import lax
from jax.experimental import pallas as pl
from jax.experimental.pallas import tpu as pltpu
from jax.sharding import Mesh
from jax.sharding import PartitionSpec as P

AXES = ("rep", "zl", "y", "x", "c")
SIZES = (2, 4, 4, 4, 2)
ZERO = AXES[1:]
TOKENS = 256


def places():
    for r in range(2):
        for zl in range(4):
            for y in range(4):
                for x in range(4):
                    for c in range(2):
                        yield r, zl, y, x, c


def rank(r, zl, y, x, c):
    return (((r * 4 + zl % 4) * 4 + y % 4) * 4 + x % 4) * 2 + c


def send(value, target):
    pairs = [(rank(*place), rank(*target(*place))) for place in places()]
    return lax.ppermute(value, AXES, pairs)


def swap_cores(value):
    return send(value, lambda r, zl, y, x, c: (r, zl, y, x, 1 - c))


def swap_reps(value):
    return send(value, lambda r, zl, y, x, c: (1 - r, zl, y, x, c))


def along_line(value, k):
    return send(value, lambda r, zl, y, x, c: (r, zl + k, y, x, c))


def first_turn(value, k):
    return send(
        value,
        lambda r, zl, y, x, c: (r, zl, y, x + k, c) if c else (r, zl, y + k, x, c),
    )


def second_turn(value, k):
    return send(
        value,
        lambda r, zl, y, x, c: (r, zl, y + k, x, c) if c else (r, zl, y, x + k, c),
    )


def to_parity(value, j, other_rep):
    def target(r, zl, y, x, c):
        return (
            r ^ other_rep,
            zl - 1 + 2 * j if c else zl - 2 * j,
            y,
            x,
            zl % 2,
        )

    return send(value, target)


def column(zl, y, x):
    return pl.multiple_of(((zl * 4 + y) * 4 + x) * 128, 128)


def back(at, k):
    return lax.rem(at + 4 - k, 4)


def arrange(where, act_rows, grad_rows, mine, other):
    zl, y, x, core = (where[i] for i in range(4))

    def write(rows, out, role):
        for k in range(4):
            for k2 in range(4):
                for kz in range(4):
                    if role == 0:
                        at = column(back(zl, kz), back(y, k2), lax.rem(x + k, 4))
                    else:
                        at = column(back(zl, kz), lax.rem(y + k, 4), back(x, k2))
                    b = (k2 * 4 + kz) * 128
                    out[k, :, b : b + 128] = rows[:, pl.ds(at, 128)]

    @pl.when(core == 0)
    def _():
        write(act_rows, mine, 0)
        write(grad_rows, other, 1)

    @pl.when(core == 1)
    def _():
        write(grad_rows, mine, 1)
        write(act_rows, other, 0)


def partials(w0, w1, w2, w3, plane, p0, p1, p2, p3):
    x = plane[...].reshape(2048, 128)
    for w, p in ((w0, p0), (w3, p1), (w2, p2), (w1, p3)):
        p[...] = jnp.dot(
            w[...].reshape(128, 2048), x, preferred_element_type=jnp.float32
        )


def tiles(g0, g1, g2, g3, plane, e0, e1, e2, e3):
    x = plane[...].reshape(1024, 256)
    for g, e in ((g0, e0), (g3, e1), (g2, e2), (g1, e3)):
        part = lax.dot_general(
            g[...], x, (((1,), (1,)), ((), ())), preferred_element_type=jnp.float32
        )
        e[...] = (part * (1.0 / TOKENS)).astype(e.dtype)


def assemble(where, own, sibling, out):
    zl, y, x, core = (where[i] for i in range(4))
    for side, piece in enumerate((own, sibling)):
        held_by = core if side == 0 else 1 - core
        match = lax.rem(zl + held_by, 2) == 0
        for k3 in range(4):
            for k2 in range(4):
                for j in range(2):
                    z = jnp.where(
                        match, lax.rem(zl + 2 * j, 4), lax.rem(zl + 5 - 2 * j, 4)
                    )
                    at = jnp.where(
                        held_by == 0,
                        column(z, back(y, k2), back(x, k3)),
                        column(z, back(y, k3), back(x, k2)),
                    )
                    b = (k2 * 2 + j) * 128
                    out[:, pl.ds(pl.multiple_of(at, 128), 128)] = piece[
                        k3, :, b : b + 128
                    ].astype(jnp.float32)


VMEM = pl.BlockSpec(memory_space=pltpu.VMEM)
SMEM = pl.BlockSpec(memory_space=pltpu.SMEM)
PARAMS = pltpu.CompilerParams(vmem_limit_bytes=40 * 1024 * 1024)


def call(body, name, shapes, ins):
    return pl.pallas_call(
        body,
        out_shape=shapes,
        in_specs=ins,
        out_specs=jax.tree.map(lambda _: VMEM, shapes),
        compiler_params=PARAMS,
        name=name,
    )


def on_device(acts, grads_out, act_inverse, grad_inverse):
    bf16, f32 = jnp.bfloat16, jnp.float32
    shape = jax.ShapeDtypeStruct
    c = lax.axis_index("c")
    where = jnp.stack(
        [lax.axis_index("zl"), lax.axis_index("y"), lax.axis_index("x"), c]
    ).astype(jnp.int32)
    first = c == 0

    acts_t, grads_t = acts.T, grads_out.T
    got = swap_cores(jnp.where(first, grads_t, acts_t))
    kept = jnp.where(first, acts_t, grads_t)
    block = jnp.concatenate(
        [jnp.where(first, kept, got), jnp.where(first, got, kept)], axis=0
    )
    mine, other = call(
        arrange, "arrange", [shape((4, 64, 2048), bf16)] * 2, [SMEM, VMEM, VMEM]
    )(where, act_inverse, grad_inverse)
    theirs = swap_cores(other)
    rows = [jnp.stack([mine[k], theirs[k]]) for k in range(4)]

    line = jnp.stack([block] + [along_line(block, k) for k in (1, 2, 3)])
    weights = [rows[0]] + [second_turn(rows[k], k) for k in (1, 2, 3)]
    plane = jnp.stack([line] + [first_turn(line, k) for k in (1, 2, 3)])
    parts = call(partials, "partials", [shape((128, 128), f32)] * 4, [VMEM] * 5)(
        *weights, plane
    )
    total = parts[0]
    for k in (1, 2, 3):
        total = total + second_turn(parts[k], k)
    pre = jnp.where(
        first, total, jnp.concatenate([total[64:], total[:64]], axis=0)
    ).astype(bf16)

    near = swap_cores(pre)
    act = jnp.where(first, pre, near)
    grad = jnp.where(first, near, pre)
    pair = jnp.stack(
        [
            jnp.concatenate([to_parity(act, j, 0), to_parity(act, j, 1)], axis=1)
            for j in (0, 1)
        ]
    )
    grad = jnp.concatenate([grad, swap_reps(grad)], axis=1)
    plane = jnp.stack([pair] + [first_turn(pair, k) for k in (1, 2, 3)])
    grads = [grad] + [second_turn(grad, k) for k in (1, 2, 3)]
    made = call(tiles, "tiles", [shape((128, 1024), bf16)] * 4, [VMEM] * 5)(
        *grads, plane
    )
    whole = [made[0]] + [second_turn(made[k], k) for k in (1, 2, 3)]
    low = jnp.stack([e[:64] for e in whole])
    high = jnp.stack([e[64:] for e in whole])
    own = jnp.where(first, low, high)
    sibling = swap_cores(jnp.where(first, high, low))
    return call(
        assemble, "assemble", shape((64, 8192), f32), [SMEM, VMEM, VMEM]
    )(where, own, sibling)


def solution(mesh):
    finer = Mesh(mesh.devices.reshape(SIZES), AXES)
    return jax.shard_map(
        on_device,
        mesh=finer,
        in_specs=(P("rep", ZERO), P("rep", ZERO), P(ZERO, None), P(ZERO, None)),
        out_specs=P(ZERO, None),
        check_vma=False,
    )
```

```python
import jax
import jax.numpy as jnp
from jax import lax
from jax.experimental import pallas as pl
from jax.experimental.pallas import tpu as pltpu
from jax.sharding import Mesh
from jax.sharding import PartitionSpec as P

AXES = ("rep", "zl", "y", "x", "c")
SIZES = (2, 4, 4, 4, 2)
ZERO = AXES[1:]
TOKENS = 256


def places():
    for r in range(2):
        for zl in range(4):
            for y in range(4):
                for x in range(4):
                    for c in range(2):
                        yield r, zl, y, x, c


def rank(r, zl, y, x, c):
    return (((r * 4 + zl % 4) * 4 + y % 4) * 4 + x % 4) * 2 + c


def send(value, target):
    pairs = [(rank(*place), rank(*target(*place))) for place in places()]
    return lax.ppermute(value, AXES, pairs)


def swap_cores(value):
    return send(value, lambda r, zl, y, x, c: (r, zl, y, x, 1 - c))


def swap_reps(value):
    return send(value, lambda r, zl, y, x, c: (1 - r, zl, y, x, c))


def along_line(value, k):
    return send(value, lambda r, zl, y, x, c: (r, zl + k, y, x, c))


def first_turn(value, k):
    return send(
        value,
        lambda r, zl, y, x, c: (r, zl, y, x + k, c) if c else (r, zl, y + k, x, c),
    )


def second_turn(value, k):
    return send(
        value,
        lambda r, zl, y, x, c: (r, zl, y + k, x, c) if c else (r, zl, y, x + k, c),
    )


def on_ring(value, shifts, cores):
    def target(r, zl, y, x, c):
        plane = (r * 4 + zl + shifts[c]) % 8
        return plane // 4, plane, y, x, cores[c]

    return send(value, target)


def third_pair(value, k):
    return send(
        value,
        lambda r, zl, y, x, c: (r, zl, y ^ k, x, c) if c else (r, zl, y, x ^ k, c),
    )


def column(zl, y, x):
    return pl.multiple_of(((zl * 4 + y) * 4 + x) * 128, 128)


def back(at, k):
    return lax.rem(at + 4 - k, 4)


def arrange(where, act_rows, grad_rows, mine, other):
    zl, y, x, core = (where[i] for i in range(4))

    def write(rows, out, role):
        for k in range(4):
            for k2 in range(4):
                for kz in range(4):
                    if role == 0:
                        at = column(back(zl, kz), back(y, k2), lax.rem(x + k, 4))
                    else:
                        at = column(back(zl, kz), lax.rem(y + k, 4), back(x, k2))
                    b = (k2 * 4 + kz) * 128
                    out[k, :, b : b + 128] = rows[:, pl.ds(at, 128)]

    @pl.when(core == 0)
    def _():
        write(act_rows, mine, 0)
        write(grad_rows, other, 1)

    @pl.when(core == 1)
    def _():
        write(grad_rows, mine, 1)
        write(act_rows, other, 0)


def partials(w0, w1, w2, w3, plane, p0, p1, p2, p3):
    x = plane[...].reshape(2048, 128)
    for w, p in ((w0, p0), (w3, p1), (w2, p2), (w1, p3)):
        p[...] = jnp.dot(
            w[...].reshape(128, 2048), x, preferred_element_type=jnp.float32
        )


def tiles(where, g, plane, e0, e1, e2, e3):
    x = plane[...].reshape(1024, 256)
    at = jnp.where(where[3] == 0, where[2], where[1])
    for k, e in enumerate((e0, e1, e2, e3)):
        apart = at ^ lax.rem(at + k, 4)
        part = lax.dot_general(
            g[apart ^ (apart >> 1)],
            x,
            (((1,), (1,)), ((), ())),
            preferred_element_type=jnp.float32,
        )
        e[...] = (part * (1.0 / TOKENS)).astype(e.dtype)


def assemble(where, *refs):
    zl, y, x, core = (where[i] for i in range(4))
    out = refs[-1]
    for side in range(2):
        held_by = core if side == 0 else 1 - core
        for k3 in range(4):
            piece = refs[side * 4 + k3]
            for k2 in range(4):
                for j in range(2):
                    z = lax.rem(jnp.where(held_by == 0, zl + 4 - j, zl + 1 + j), 4)
                    at = jnp.where(
                        held_by == 0,
                        column(z, back(y, k2), back(x, k3)),
                        column(z, back(y, k3), back(x, k2)),
                    )
                    b = (k2 * 2 + j) * 128
                    out[:, pl.ds(pl.multiple_of(at, 128), 128)] = piece[
                        :, b : b + 128
                    ].astype(jnp.float32)


VMEM = pl.BlockSpec(memory_space=pltpu.VMEM)
SMEM = pl.BlockSpec(memory_space=pltpu.SMEM)
PARAMS = pltpu.CompilerParams(vmem_limit_bytes=40 * 1024 * 1024)


def call(body, name, shapes, ins):
    return pl.pallas_call(
        body,
        out_shape=shapes,
        in_specs=ins,
        out_specs=jax.tree.map(lambda _: VMEM, shapes),
        compiler_params=PARAMS,
        name=name,
    )


def on_device(acts, grads_out, act_inverse, grad_inverse):
    bf16, f32 = jnp.bfloat16, jnp.float32
    shape = jax.ShapeDtypeStruct
    c = lax.axis_index("c")
    where = jnp.stack(
        [lax.axis_index("zl"), lax.axis_index("y"), lax.axis_index("x"), c]
    ).astype(jnp.int32)
    first = c == 0

    acts_t, grads_t = acts.T, grads_out.T
    to_swap = jnp.where(first, grads_t, acts_t)
    got = swap_cores(to_swap)
    kept = jnp.where(first, acts_t, grads_t)
    block = jnp.concatenate(
        [jnp.where(first, kept, got), jnp.where(first, got, kept)], axis=0
    )
    mine, other = call(
        arrange, "arrange", [shape((4, 64, 2048), bf16)] * 2, [SMEM, VMEM, VMEM]
    )(where, act_inverse, grad_inverse)
    theirs = swap_cores(other)
    rows = [jnp.stack([mine[k], theirs[k]]) for k in range(4)]
    weights = [rows[0]] + [second_turn(rows[k], k) for k in (1, 2, 3)]

    line = jnp.stack([block] + [along_line(block, k) for k in (1, 2, 3)])
    line, weights[1], weights[3] = lax.optimization_barrier(
        (line, weights[1], weights[3])
    )
    plane = jnp.stack([line] + [first_turn(line, k) for k in (1, 2, 3)])
    parts = call(partials, "partials", [shape((128, 128), f32)] * 4, [VMEM] * 5)(
        *weights, plane
    )
    total = parts[0]
    for k in (1, 2, 3):
        total = total + second_turn(parts[k], k)
    pre = jnp.where(
        first, total, jnp.concatenate([total[64:], total[:64]], axis=0)
    ).astype(bf16)

    far = swap_reps(pre)
    low_rep = lax.axis_index("rep") == 0
    pre = jnp.concatenate(
        [jnp.where(low_rep, pre, far), jnp.where(low_rep, far, pre)], axis=1
    )
    got = on_ring(pre, (-1, 0), (1, 0))
    act = jnp.where(first, pre, got)
    grad = jnp.where(first, got, pre)
    pair = jnp.stack([act, on_ring(act, (1, -1), (0, 1))])
    grads = jnp.stack([grad, third_pair(grad, 1)])
    plane = jnp.stack([pair] + [first_turn(pair, k) for k in (1, 2, 3)])
    grads = jnp.concatenate([grads, third_pair(grads, 3)], axis=0)
    made = call(
        tiles, "tiles", [shape((128, 1024), bf16)] * 4, [SMEM, VMEM, VMEM]
    )(where, grads, plane)
    whole = [made[0]] + [second_turn(made[k], k) for k in (1, 2, 3)]
    own = [jnp.where(first, e[:64], e[64:]) for e in whole]
    sibling = [swap_cores(jnp.where(first, e[64:], e[:64])) for e in whole]
    return call(
        assemble, "assemble", shape((64, 8192), f32), [SMEM] + [VMEM] * 8
    )(where, *own, *sibling)


def solution(mesh):
    finer = Mesh(mesh.devices.reshape(SIZES), AXES)
    return jax.shard_map(
        on_device,
        mesh=finer,
        in_specs=(P("rep", ZERO), P("rep", ZERO), P(ZERO, None), P(ZERO, None)),
        out_specs=P(ZERO, None),
        check_vma=False,
    )
```

```python
import functools

import jax
import jax.numpy as jnp
from jax import lax
from jax.experimental import pallas as pl
from jax.experimental.pallas import tpu as pltpu
from jax.sharding import Mesh
from jax.sharding import PartitionSpec as P

AXES = ("rep", "zl", "y", "x", "c")
SIZES = (2, 4, 4, 4, 2)
ZERO = AXES[1:]
TOKENS = 256


def places():
    for r in range(2):
        for zl in range(4):
            for y in range(4):
                for x in range(4):
                    for c in range(2):
                        yield r, zl, y, x, c


def rank(r, zl, y, x, c):
    return (((r * 4 + zl % 4) * 4 + y % 4) * 4 + x % 4) * 2 + c


def send(value, target):
    pairs = [(rank(*place), rank(*target(*place))) for place in places()]
    return lax.ppermute(value, AXES, pairs)


def swap_cores(value):
    return send(value, lambda r, zl, y, x, c: (r, zl, y, x, 1 - c))


def along_line(value, k):
    return send(value, lambda r, zl, y, x, c: (r, zl ^ k, y, x, c))


def first_turn(value, k):
    return send(
        value,
        lambda r, zl, y, x, c: (r, zl, y, x + k, c) if c else (r, zl, y + k, x, c),
    )


def second_turn(value, k):
    return send(
        value,
        lambda r, zl, y, x, c: (r, zl, y + k, x, c) if c else (r, zl, y, x + k, c),
    )


def on_ring(value, shifts, cores):
    def target(r, zl, y, x, c):
        plane = (r * 4 + zl + shifts[c]) % 8
        return plane // 4, plane, y, x, cores[c]

    return send(value, target)


def turned(turn, values):
    got = {k: turn(values[k], k) for k in (1, 3, 2)}
    return [values[0]] + [got[k] for k in (1, 2, 3)]


def third_pair(value, k):
    return send(
        value,
        lambda r, zl, y, x, c: (r, zl, y ^ k, x, c) if c else (r, zl, y, x ^ k, c),
    )


def column(zl, y, x):
    return pl.multiple_of(((zl * 4 + y) * 4 + x) * 128, 128)


def back(at, k):
    return lax.rem(at + 4 - k, 4)


def arrange(where, act_hbm, grad_hbm, mine, other, act_rows, grad_rows, sems):
    zl, y, x, core = (where[i] for i in range(4))
    copies = []
    for n, (far, near) in enumerate(((act_hbm, act_rows), (grad_hbm, grad_rows))):
        for i in range(4):
            part = pl.ds(i * 16, 16)
            copies.append(
                pltpu.make_async_copy(far.at[part], near.at[part], sems.at[n * 4 + i])
            )
    for copy in copies:
        copy.start()
    for copy in copies:
        copy.wait()

    def write(rows, out, role):
        for k in range(4):
            for k2 in range(4):
                for kz in range(4):
                    if role == 0:
                        at = column(zl ^ kz, back(y, k2), lax.rem(x + k, 4))
                    else:
                        at = column(zl ^ kz, lax.rem(y + k, 4), back(x, k2))
                    b = (k2 * 4 + kz) * 128
                    out[k, :, b : b + 128] = rows[:, pl.ds(at, 128)]

    @pl.when(core == 0)
    def _():
        write(act_rows, mine, 0)
        write(grad_rows, other, 1)

    @pl.when(core == 1)
    def _():
        write(grad_rows, mine, 1)
        write(act_rows, other, 0)


def partials(w0, w1, w2, w3, plane, p0, p1, p2, p3):
    x = plane[...].reshape(2048, 128)
    for w, p in ((w0, p0), (w3, p1), (w2, p2), (w1, p3)):
        p[...] = jnp.dot(
            w[...].reshape(128, 2048), x, preferred_element_type=jnp.float32
        )


def tiles(where, g, plane, e0, e1, e2, e3):
    x = plane[...].reshape(1024, 256)
    at = jnp.where(where[3] == 0, where[2], where[1])
    for k, e in enumerate((e0, e1, e2, e3)):
        apart = at ^ lax.rem(at + k, 4)
        part = lax.dot_general(
            g[apart ^ (apart >> 1)],
            x,
            (((1,), (1,)), ((), ())),
            preferred_element_type=jnp.float32,
        )
        e[...] = (part * (1.0 / TOKENS)).astype(e.dtype)


def place(sides, where, *refs):
    zl, y, x, core = (where[i] for i in range(4))
    pieces, (out, wide, sems) = refs[: len(sides)], refs[-3:]
    copies = []
    for (side, k3), piece in zip(sides, pieces):
        held_by = core if side == 0 else 1 - core
        for k2 in range(4):
            for j in range(2):
                z = lax.rem(zl + 4 - j - 2 * held_by, 4)
                at = jnp.where(
                    held_by == 0,
                    column(z, back(y, k2), back(x, k3)),
                    column(z, back(y, k3), back(x, k2)),
                )
                b, n = (k2 * 2 + j) * 128, len(copies)
                wide[n] = piece[:, b : b + 128].astype(jnp.float32)
                copy = pltpu.make_async_copy(
                    wide.at[n],
                    out.at[:, pl.ds(pl.multiple_of(at, 128), 128)],
                    sems.at[n],
                )
                copy.start()
                copies.append(copy)
    for copy in copies:
        copy.wait()


VMEM = pl.BlockSpec(memory_space=pltpu.VMEM)
SMEM = pl.BlockSpec(memory_space=pltpu.SMEM)
HBM = pl.BlockSpec(memory_space=pltpu.HBM)
PARAMS = pltpu.CompilerParams(vmem_limit_bytes=40 * 1024 * 1024)


def call(body, name, shapes, ins, scratch=()):
    return pl.pallas_call(
        body,
        out_shape=shapes,
        in_specs=ins,
        out_specs=jax.tree.map(lambda _: VMEM, shapes),
        scratch_shapes=scratch,
        compiler_params=PARAMS,
        name=name,
    )


def placed(where, out, pieces):
    sides, values = list(pieces), list(pieces.values())
    n = 8 * len(sides)
    held = [] if out is None else [out]
    return pl.pallas_call(
        functools.partial(place, sides),
        out_shape=jax.ShapeDtypeStruct((64, 8192), jnp.float32),
        in_specs=[SMEM] + [VMEM] * len(sides) + [HBM] * len(held),
        out_specs=HBM,
        scratch_shapes=[
            pltpu.VMEM((n, 64, 128), jnp.float32),
            pltpu.SemaphoreType.DMA((n,)),
        ],
        input_output_aliases={1 + len(sides): 0} if held else {},
        compiler_params=PARAMS,
        name="place",
    )(where, *values, *held)


def on_device(acts, grads_out, act_inverse, grad_inverse):
    bf16, f32 = jnp.bfloat16, jnp.float32
    shape = jax.ShapeDtypeStruct
    c = lax.axis_index("c")
    where = jnp.stack(
        [lax.axis_index("zl"), lax.axis_index("y"), lax.axis_index("x"), c]
    ).astype(jnp.int32)
    first = c == 0

    acts_t, grads_t = acts.T, grads_out.T
    to_swap = jnp.where(first, grads_t, acts_t)
    got = swap_cores(to_swap)
    kept = jnp.where(first, acts_t, grads_t)
    block = jnp.concatenate(
        [jnp.where(first, kept, got), jnp.where(first, got, kept)], axis=0
    )
    mine, other = call(
        arrange, "arrange", [shape((4, 64, 2048), bf16)] * 2, [SMEM, HBM, HBM],
        [pltpu.VMEM((64, 8192), bf16)] * 2 + [pltpu.SemaphoreType.DMA((8,))],
    )(where, act_inverse, grad_inverse)
    theirs = swap_cores(other)
    rows = [jnp.stack([mine[k], theirs[k]]) for k in range(4)]
    weights = turned(second_turn, rows)

    line = jnp.stack([block, along_line(block, 1)])
    line = jnp.concatenate([line, along_line(line, 2)], axis=0)
    line, weights[1], weights[3] = lax.optimization_barrier(
        (line, weights[1], weights[3])
    )
    plane = jnp.stack(turned(first_turn, [line] * 4))
    parts = call(partials, "partials", [shape((128, 128), f32)] * 4, [VMEM] * 5)(
        *weights, plane
    )
    total = sum(turned(second_turn, parts))
    pre = jnp.where(
        first, total, jnp.concatenate([total[64:], total[:64]], axis=0)
    ).astype(bf16)

    r, zl = lax.axis_index("rep"), where[0]
    got = on_ring(pre, (-1, 1), (1, 0))
    act = jnp.where(first, pre, got)
    one = on_ring(jnp.stack([act, got]), (1, -1), (0, 1))
    two = on_ring(jnp.concatenate([act[None], one], axis=0), (2, -2), (0, 1))
    cross = swap_cores(
        jnp.where(first, two, jnp.stack([two[1], two[0], pre]))
    )
    near = (jnp.where(first, act, cross[0]), jnp.where(first, one[0], cross[1]))
    over = (jnp.where(first, cross[0], one[0]), jnp.where(first, cross[1], act))

    def by_rep(low, a, b):
        return jnp.concatenate([jnp.where(low, a, b), jnp.where(low, b, a)], axis=1)

    pair = jnp.stack(
        [by_rep((r == 0) == (zl >= j + 2 * c), near[j], over[j]) for j in (0, 1)]
    )
    grad = by_rep(
        r == 0, jnp.where(first, cross[2], pre), jnp.where(first, two[2], cross[2])
    )
    grads = jnp.stack([grad, third_pair(grad, 1)])
    plane = jnp.stack(turned(first_turn, [pair] * 4))
    grads = jnp.concatenate([grads, third_pair(grads, 3)], axis=0)
    made = call(
        tiles, "tiles", [shape((128, 1024), bf16)] * 4, [SMEM, VMEM, VMEM]
    )(where, grads, plane)
    whole = turned(second_turn, made)

    def parted(e):
        return jnp.where(first, e[:64], e[64:]), jnp.where(first, e[64:], e[:64])

    own, give = zip(*(parted(e) for e in whole))
    give, sibling = list(give), {}
    sibling[0] = swap_cores(give[0])
    out = placed(where, None, {(0, 0): own[0], (1, 0): sibling[0]})
    sibling[3] = swap_cores(give[3])
    give[2], out = lax.optimization_barrier((give[2], out))
    sibling[2] = swap_cores(give[2])
    out = placed(where, out, {(0, 3): own[3], (1, 3): sibling[3], (0, 2): own[2]})
    give[1], out = lax.optimization_barrier((give[1], out))
    sibling[1] = swap_cores(give[1])
    out = placed(where, out, {(0, 1): own[1], (1, 2): sibling[2]})
    return placed(where, out, {(1, 1): sibling[1]})


def solution(mesh):
    finer = Mesh(mesh.devices.reshape(SIZES), AXES)
    return jax.shard_map(
        on_device,
        mesh=finer,
        in_specs=(P("rep", ZERO), P("rep", ZERO), P(ZERO, None), P(ZERO, None)),
        out_specs=P(ZERO, None),
        check_vma=False,
    )
```

```python
import jax
import jax.numpy as jnp
from jax import lax
from jax.experimental import pallas as pl
from jax.experimental.pallas import tpu as pltpu
from jax.sharding import Mesh
from jax.sharding import PartitionSpec as P

AXES = ("rep", "zl", "y", "x", "c")
SIZES = (2, 4, 4, 4, 2)
ZERO = AXES[1:]
TOKENS = 256


def places():
    for r in range(2):
        for zl in range(4):
            for y in range(4):
                for x in range(4):
                    for c in range(2):
                        yield r, zl, y, x, c


def rank(r, zl, y, x, c):
    return (((r * 4 + zl) * 4 + y) * 4 + x) * 2 + c


def send(value, target):
    pairs = [(rank(*place), rank(*target(*place))) for place in places()]
    return lax.ppermute(value, AXES, pairs)


def swap_cores(value):
    return send(value, lambda r, zl, y, x, c: (r, zl, y, x, 1 - c))


def along_line(value, k):
    return send(value, lambda r, zl, y, x, c: (r, zl ^ k, y, x, c))


def first_turn(value, k):
    return send(
        value,
        lambda r, zl, y, x, c: (r, zl, y, x ^ k, c) if c else (r, zl, y ^ k, x, c),
    )


def second_turn(value, k):
    return send(
        value,
        lambda r, zl, y, x, c: (r, zl, y ^ k, x, c) if c else (r, zl, y, x ^ k, c),
    )


def turned(turn, values):
    got = {k: turn(values[k], k) for k in (1, 3, 2)}
    return [values[0]] + [got[k] for k in (1, 2, 3)]


def column(where, core, k3, k2, z):
    y = where[1] ^ jnp.where(core == 0, k2, k3)
    x = where[2] ^ jnp.where(core == 0, k3, k2)
    return pl.multiple_of(((z * 4 + y) * 4 + x) * 128, 128)


def product(where, turns, pieces, mine, theirs):
    total = jnp.zeros((128, 128), jnp.float32)
    for k3, piece in zip(turns, pieces):
        for k2 in range(4):
            at = [
                pl.ds(column(where, where[3], k3, k2, where[0] ^ kz), 128)
                for kz in range(4)
            ]
            rows = jnp.concatenate(
                [
                    jnp.concatenate([side[:, part] for part in at], axis=1)
                    for side in (mine, theirs)
                ],
                axis=0,
            )
            total += jnp.dot(
                rows,
                piece[k2].reshape(512, 128),
                preferred_element_type=jnp.float32,
            )
    return total


def sums_most(where, p0, p1, p2, mine, theirs, total):
    total[...] = product(where, EARLY, (p0, p1, p2), mine, theirs)


def sums_rest(where, p3, mine, theirs, most, pre):
    total = most[...] + product(where, LATE, (p3,), mine, theirs)
    crossed = jnp.concatenate([total[64:], total[:64]], axis=0)
    pre[...] = jnp.where(where[3] == 0, total, crossed).astype(pre.dtype)


EARLY, LATE = (0, 2, 3), (1,)


def tiles(g, plane, *made):
    x = plane[...].reshape(1024, 256)
    for k, e in enumerate(made):
        part = lax.dot_general(
            g[k ^ (k >> 1)],
            x,
            (((1,), (1,)), ((), ())),
            preferred_element_type=jnp.float32,
        )
        e[...] = (part * (1.0 / TOKENS)).astype(e.dtype)


def assemble(where, *refs):
    core, out = where[3], refs[-1]
    for side in range(2):
        held_by = core if side == 0 else 1 - core
        for k3 in range(4):
            piece = refs[side * 4 + k3]
            for k2 in range(4):
                for j in range(2):
                    at = column(where, held_by, k3, k2, j + 2 * held_by)
                    b = (k2 * 2 + j) * 128
                    out[:, pl.ds(at, 128)] = piece[:, b : b + 128].astype(jnp.float32)


VMEM = pl.BlockSpec(memory_space=pltpu.VMEM)
SMEM = pl.BlockSpec(memory_space=pltpu.SMEM)
PARAMS = pltpu.CompilerParams(vmem_limit_bytes=40 * 1024 * 1024)


def call(body, name, shapes, ins):
    return pl.pallas_call(
        body,
        out_shape=shapes,
        in_specs=ins,
        out_specs=jax.tree.map(lambda _: VMEM, shapes),
        compiler_params=PARAMS,
        name=name,
    )


def on_device(acts, grads_out, act_inverse, grad_inverse):
    bf16, f32 = jnp.bfloat16, jnp.float32
    shape = jax.ShapeDtypeStruct
    c = lax.axis_index("c")
    where = jnp.stack(
        [lax.axis_index("zl"), lax.axis_index("y"), lax.axis_index("x"), c]
    ).astype(jnp.int32)
    first = c == 0

    acts_t, grads_t = acts.T, grads_out.T
    got = swap_cores(jnp.where(first, grads_t, acts_t))
    kept = jnp.where(first, acts_t, grads_t)
    block = jnp.concatenate(
        [jnp.where(first, kept, got), jnp.where(first, got, kept)], axis=0
    )
    line = jnp.stack(turned(along_line, [block] * 4))
    rows = turned(first_turn, [line] * 4)
    rows[1], act_inverse, grad_inverse = lax.optimization_barrier(
        (rows[1], act_inverse, grad_inverse)
    )
    theirs = swap_cores(jnp.where(first, grad_inverse, act_inverse))
    mine = jnp.where(first, act_inverse, grad_inverse)
    plane = jnp.stack(rows)
    pieces = turned(second_turn, [plane] * 4)
    most = call(
        sums_most, "sums_most", shape((128, 128), f32), [SMEM] + [VMEM] * 5
    )(where, *(pieces[k] for k in EARLY), mine, theirs)
    pre = call(
        sums_rest, "sums_rest", shape((128, 128), bf16), [SMEM] + [VMEM] * 4
    )(where, *(pieces[k] for k in LATE), mine, theirs, most)

    sent = jnp.broadcast_to(pre, (8, 128, 128))
    all_planes = lax.all_to_all(sent, ("rep", "zl"), 0, 0, tiled=True)
    all_planes = all_planes.reshape(2, 4, 128, 128)
    here = lax.dynamic_slice_in_dim(all_planes, where[0], 1, axis=1)
    cross = swap_cores(
        jnp.where(first, all_planes[:, 2:], jnp.concatenate([here, here], axis=1))
    )
    pair = jnp.where(first, all_planes[:, :2], cross)
    pair = jnp.concatenate([pair[0], pair[1]], axis=2)
    grad = jnp.where(first, cross[:, 0], here[:, 0])
    grad = jnp.concatenate([grad[0], grad[1]], axis=1)

    grads = jnp.stack([grad, second_turn(grad, 1)])
    plane = jnp.stack(turned(first_turn, [pair] * 4))
    grads = jnp.concatenate([grads, second_turn(grads, 3)], axis=0)
    made = call(tiles, "tiles", [shape((128, 1024), bf16)] * 4, [VMEM] * 2)(
        grads, plane
    )
    whole = turned(second_turn, made)
    own = [jnp.where(first, e[:64], e[64:]) for e in whole]
    sibling = [swap_cores(jnp.where(first, e[64:], e[:64])) for e in whole]
    return call(
        assemble, "assemble", shape((64, 8192), f32), [SMEM] + [VMEM] * 8
    )(where, *own, *sibling)


def solution(mesh):
    finer = Mesh(mesh.devices.reshape(SIZES), AXES)
    return jax.shard_map(
        on_device,
        mesh=finer,
        in_specs=(P("rep", ZERO), P("rep", ZERO), P(ZERO, None), P(ZERO, None)),
        out_specs=P(ZERO, None),
        check_vma=False,
    )
```

```python
import jax
import jax.numpy as jnp
from jax import lax
from jax.experimental import pallas as pl
from jax.experimental.pallas import tpu as pltpu
from jax.sharding import Mesh
from jax.sharding import PartitionSpec as P

AXES = ("rep", "zl", "y", "x", "c")
SIZES = (2, 4, 4, 4, 2)
ZERO = AXES[1:]
TOKENS = 256


def places():
    for r in range(2):
        for zl in range(4):
            for y in range(4):
                for x in range(4):
                    for c in range(2):
                        yield r, zl, y, x, c


def rank(r, zl, y, x, c):
    return (((r * 4 + zl) * 4 + y) * 4 + x) * 2 + c


def send(value, target):
    pairs = [(rank(*place), rank(*target(*place))) for place in places()]
    return lax.ppermute(value, AXES, pairs)


def swap_cores(value):
    return send(value, lambda r, zl, y, x, c: (r, zl, y, x, 1 - c))


def along_line(value, k):
    return send(value, lambda r, zl, y, x, c: (r, zl ^ k, y, x, c))


def first_turn(value, k):
    return send(
        value,
        lambda r, zl, y, x, c: (r, zl, y, x ^ k, c) if c else (r, zl, y ^ k, x, c),
    )


def second_turn(value, k):
    return send(
        value,
        lambda r, zl, y, x, c: (r, zl, y ^ k, x, c) if c else (r, zl, y, x ^ k, c),
    )


def to_parity(value, j, other_rep):
    def target(r, zl, y, x, c):
        return r ^ other_rep, zl ^ (2 * j + c), y, x, zl % 2

    return send(value, target)


def turned(turn, values):
    got = {k: turn(values[k], k) for k in (1, 3, 2)}
    return [values[0]] + [got[k] for k in (1, 2, 3)]


def column(where, core, k3, k2, z):
    k_y, k_x = (k2, k3), (k3, k2)
    if isinstance(core, int):
        y, x = where[1] ^ k_y[core], where[2] ^ k_x[core]
    else:
        y = where[1] ^ jnp.where(core == 0, *k_y)
        x = where[2] ^ jnp.where(core == 0, *k_x)
    return pl.multiple_of(((z * 4 + y) * 4 + x) * 128, 128)


def precondition(where, p0, p1, p2, p3, act_rows, grad_rows, acts_there, grads_there, pre):
    def product(core, mine, theirs):
        total = jnp.zeros((128, 128), jnp.float32)
        for k3, piece in enumerate((p0, p1, p2, p3)):
            for k2 in range(4):
                at = [
                    pl.ds(column(where, core, k3, k2, where[0] ^ kz), 128)
                    for kz in range(4)
                ]
                rows = jnp.concatenate(
                    [
                        jnp.concatenate([side[:, part] for part in at], axis=1)
                        for side in (mine, theirs)
                    ],
                    axis=0,
                )
                total += jnp.dot(
                    rows,
                    piece[k2].reshape(512, 128),
                    preferred_element_type=jnp.float32,
                )
        return total.astype(pre.dtype)

    @pl.when(where[3] == 0)
    def _():
        pre[...] = product(0, act_rows, acts_there)

    @pl.when(where[3] == 1)
    def _():
        pre[...] = product(1, grads_there, grad_rows)


def tiles(g, plane, *made):
    x = plane[...].reshape(1024, 256)
    for k, e in enumerate(made):
        part = lax.dot_general(
            g[k ^ (k >> 1)],
            x,
            (((1,), (1,)), ((), ())),
            preferred_element_type=jnp.float32,
        )
        e[...] = (part * (1.0 / TOKENS)).astype(e.dtype)


def assemble(where, *refs):
    core, out = where[3], refs[-1]
    for side in range(2):
        held_by = core if side == 0 else 1 - core
        for k3 in range(4):
            piece = refs[side * 4 + k3]
            for k2 in range(4):
                for j in range(2):
                    z = where[0] ^ (2 * j + lax.rem(where[0] + held_by, 2))
                    at = column(where, held_by, k3, k2, z)
                    b = (k2 * 2 + j) * 128
                    out[:, pl.ds(at, 128)] = piece[:, b : b + 128].astype(jnp.float32)


VMEM = pl.BlockSpec(memory_space=pltpu.VMEM)
SMEM = pl.BlockSpec(memory_space=pltpu.SMEM)
PARAMS = pltpu.CompilerParams(vmem_limit_bytes=40 * 1024 * 1024)


def call(body, name, shapes, ins):
    return pl.pallas_call(
        body,
        out_shape=shapes,
        in_specs=ins,
        out_specs=jax.tree.map(lambda _: VMEM, shapes),
        compiler_params=PARAMS,
        name=name,
    )


def on_device(acts, grads_out, act_inverse, grad_inverse):
    bf16, f32 = jnp.bfloat16, jnp.float32
    shape = jax.ShapeDtypeStruct
    c = lax.axis_index("c")
    where = jnp.stack(
        [lax.axis_index("zl"), lax.axis_index("y"), lax.axis_index("x"), c]
    ).astype(jnp.int32)
    first = c == 0

    acts_t, grads_t = acts.T, grads_out.T
    got = swap_cores(jnp.where(first, grads_t, acts_t))
    kept = jnp.where(first, acts_t, grads_t)
    block = jnp.concatenate(
        [jnp.where(first, kept, got), jnp.where(first, got, kept)], axis=0
    )
    line = jnp.stack(turned(along_line, [block] * 4))
    plane = jnp.stack(turned(first_turn, [line] * 4))
    pieces = turned(second_turn, [plane] * 4)
    pre = call(
        precondition, "precondition", shape((128, 128), bf16), [SMEM] + [VMEM] * 8
    )(
        where,
        *pieces,
        act_inverse,
        grad_inverse,
        swap_cores(act_inverse),
        swap_cores(grad_inverse),
    )

    near = swap_cores(pre)
    act = jnp.where(first, pre, near)
    grad = jnp.where(first, near, pre)
    riding = to_parity(jnp.stack([act, grad]), 0, 1)
    there = (riding[0], to_parity(act, 1, 1))
    here = [to_parity(act, j, 0) for j in (1, 0)][::-1]
    pair = jnp.stack([jnp.concatenate(p, axis=1) for p in zip(here, there)])
    far = jnp.where(
        lax.rem(where[0] + c, 2) == 0, riding[1], swap_cores(riding[1])
    )
    grad = jnp.concatenate([grad, far], axis=1)

    grads = jnp.stack([grad, second_turn(grad, 1)])
    plane = jnp.stack(turned(first_turn, [pair] * 4))
    grads = jnp.concatenate([grads, second_turn(grads, 3)], axis=0)
    made = call(tiles, "tiles", [shape((128, 1024), bf16)] * 4, [VMEM] * 2)(
        grads, plane
    )
    whole = turned(second_turn, made)
    own = [jnp.where(first, e[:64], e[64:]) for e in whole]
    sibling = [swap_cores(jnp.where(first, e[64:], e[:64])) for e in whole]
    return call(
        assemble, "assemble", shape((64, 8192), f32), [SMEM] + [VMEM] * 8
    )(where, *own, *sibling)


def solution(mesh):
    finer = Mesh(mesh.devices.reshape(SIZES), AXES)
    return jax.shard_map(
        on_device,
        mesh=finer,
        in_specs=(P("rep", ZERO), P("rep", ZERO), P(ZERO, None), P(ZERO, None)),
        out_specs=P(ZERO, None),
        check_vma=False,
    )
```

```python
import jax
import jax.numpy as jnp
from jax import lax
from jax.experimental import pallas as pl
from jax.experimental.pallas import tpu as pltpu
from jax.sharding import Mesh
from jax.sharding import PartitionSpec as P

AXES = ("rep", "zl", "y", "x", "c")
SIZES = (2, 4, 4, 4, 2)
ZERO = AXES[1:]
TOKENS = 256


def places():
    for r in range(2):
        for zl in range(4):
            for y in range(4):
                for x in range(4):
                    for c in range(2):
                        yield r, zl, y, x, c


def rank(r, zl, y, x, c):
    return (((r * 4 + zl) * 4 + y) * 4 + x) * 2 + c


def send(value, target):
    pairs = [(rank(*place), rank(*target(*place))) for place in places()]
    return lax.ppermute(value, AXES, pairs)


def swap_cores(value):
    return send(value, lambda r, zl, y, x, c: (r, zl, y, x, 1 - c))


def swap_reps(value):
    return send(value, lambda r, zl, y, x, c: (1 - r, zl, y, x, c))


def along_line(value, k):
    return send(value, lambda r, zl, y, x, c: (r, zl ^ k, y, x, c))


def first_turn(value, k):
    return send(
        value,
        lambda r, zl, y, x, c: (r, zl, y, x ^ k, c) if c else (r, zl, y ^ k, x, c),
    )


def second_turn(value, k):
    return send(
        value,
        lambda r, zl, y, x, c: (r, zl, y ^ k, x, c) if c else (r, zl, y, x ^ k, c),
    )


def to_parity(value, j, other_rep):
    def target(r, zl, y, x, c):
        return r ^ other_rep, zl ^ (2 * j + c), y, x, zl % 2

    return send(value, target)


def turned(turn, values):
    got = {k: turn(values[k], k) for k in (1, 3, 2)}
    return [values[0]] + [got[k] for k in (1, 2, 3)]


def column(where, core, k3, k2, z):
    y = where[1] ^ jnp.where(core == 0, k2, k3)
    x = where[2] ^ jnp.where(core == 0, k3, k2)
    return pl.multiple_of(((z * 4 + y) * 4 + x) * 128, 128)


def precondition(where, p0, p1, p2, p3, mine, theirs, pre):
    total = jnp.zeros((128, 128), jnp.float32)
    for k3, piece in enumerate((p0, p1, p2, p3)):
        for k2 in range(4):
            at = [
                pl.ds(column(where, where[3], k3, k2, where[0] ^ kz), 128)
                for kz in range(4)
            ]
            rows = jnp.concatenate(
                [
                    jnp.concatenate([side[:, part] for part in at], axis=1)
                    for side in (mine, theirs)
                ],
                axis=0,
            )
            total += jnp.dot(
                rows,
                piece[k2].reshape(512, 128),
                preferred_element_type=jnp.float32,
            )
    crossed = jnp.concatenate([total[64:], total[:64]], axis=0)
    pre[...] = jnp.where(where[3] == 0, total, crossed).astype(pre.dtype)


def tiles(g, plane, *made):
    x = plane[...].reshape(1024, 256)
    for k, e in enumerate(made):
        part = lax.dot_general(
            g[k ^ (k >> 1)],
            x,
            (((1,), (1,)), ((), ())),
            preferred_element_type=jnp.float32,
        )
        e[...] = (part * (1.0 / TOKENS)).astype(e.dtype)


FIRST = 1


def assemble(where, *refs):
    pieces, (out, wide, sems) = refs[:8], refs[8:]
    core = where[3]
    places = []
    for side in range(2):
        held_by = core if side == 0 else 1 - core
        for k3 in range(4):
            for k2 in range(4):
                for j in range(2):
                    z = where[0] ^ (2 * j + lax.rem(where[0] + held_by, 2))
                    at = column(where, held_by, k3, k2, z)
                    places.append((pieces[side * 4 + k3], (k2 * 2 + j) * 128, at))
    copies = []
    for i in range(4):
        rows = slice(i * 16, i * 16 + 16)
        for piece, b, at in places:
            wide[rows, pl.ds(at, 128)] = piece[rows, b : b + 128].astype(jnp.float32)
        copies.append(pltpu.make_async_copy(wide.at[rows], out.at[rows], sems.at[i]))
        copies[-1].start()
    for copy in copies:
        copy.wait()


VMEM = pl.BlockSpec(memory_space=pltpu.VMEM)
SMEM = pl.BlockSpec(memory_space=pltpu.SMEM)
PARAMS = pltpu.CompilerParams(vmem_limit_bytes=12 * 1024 * 1024)


def call(body, name, shapes, ins):
    return pl.pallas_call(
        body,
        out_shape=shapes,
        in_specs=ins,
        out_specs=jax.tree.map(lambda _: VMEM, shapes),
        compiler_params=PARAMS,
        name=name,
    )


def on_device(acts, grads_out, act_inverse, grad_inverse):
    bf16, f32 = jnp.bfloat16, jnp.float32
    shape = jax.ShapeDtypeStruct
    c = lax.axis_index("c")
    where = jnp.stack(
        [lax.axis_index("zl"), lax.axis_index("y"), lax.axis_index("x"), c]
    ).astype(jnp.int32)
    first = c == 0

    acts_t, grads_t = acts.T, grads_out.T
    kept, given = lax.optimization_barrier(
        (jnp.where(first, acts_t, grads_t), jnp.where(first, grads_t, acts_t))
    )
    got = swap_cores(given)
    block = jnp.concatenate(
        [jnp.where(first, kept, got), jnp.where(first, got, kept)], axis=0
    )
    mine = jnp.where(first, act_inverse, grad_inverse)
    theirs = jnp.where(first, swap_cores(act_inverse), swap_cores(grad_inverse))
    line = jnp.stack(turned(along_line, [block] * 4))
    plane = jnp.stack(turned(first_turn, [line] * 4))
    pieces = turned(second_turn, [plane] * 4)
    pre = call(
        precondition, "precondition", shape((128, 128), bf16), [SMEM] + [VMEM] * 6
    )(where, *pieces, mine, theirs)

    near = swap_cores(pre)
    act = jnp.where(first, pre, near)
    grad = jnp.where(first, near, pre)
    here = [to_parity(act, j, 0) for j in (0, 1)]
    there = [to_parity(act, j, 1) for j in (0, 1)]
    pair = jnp.stack([jnp.concatenate(p, axis=1) for p in zip(here, there)])
    grad = jnp.concatenate([grad, swap_reps(grad)], axis=1)

    grads = jnp.stack([grad, second_turn(grad, 1)])
    plane = jnp.stack(turned(first_turn, [pair] * 4))
    grads = jnp.concatenate([grads, second_turn(grads, 3)], axis=0)
    made = call(tiles, "tiles", [shape((128, 1024), bf16)] * 4, [VMEM] * 2)(
        grads, plane
    )
    whole = turned(second_turn, made)
    own = [jnp.where(first, e[:64], e[64:]) for e in whole]
    give = [jnp.where(first, e[64:], e[:64]) for e in whole]
    one = swap_cores(jnp.stack([give[0], give[FIRST]]))
    sibling = {0: one[0], FIRST: one[1]}
    for k in (1, 2, 3):
        if k != FIRST:
            sibling[k] = swap_cores(give[k])
    return pl.pallas_call(
        assemble,
        out_shape=shape((64, 8192), f32),
        in_specs=[SMEM] + [VMEM] * 8,
        out_specs=pl.BlockSpec(memory_space=pltpu.HBM),
        scratch_shapes=[pltpu.VMEM((64, 8192), f32), pltpu.SemaphoreType.DMA((4,))],
        compiler_params=PARAMS,
        name="assemble",
    )(where, *own, *(sibling[k] for k in range(4)))


def solution(mesh):
    finer = Mesh(mesh.devices.reshape(SIZES), AXES)
    return jax.shard_map(
        on_device,
        mesh=finer,
        in_specs=(P("rep", ZERO), P("rep", ZERO), P(ZERO, None), P(ZERO, None)),
        out_specs=P(ZERO, None),
        check_vma=False,
    )
```

```python
import jax
import jax.numpy as jnp
from jax import lax
from jax.experimental import pallas as pl
from jax.experimental.pallas import tpu as pltpu
from jax.sharding import Mesh
from jax.sharding import PartitionSpec as P

AXES = ("rep", "zl", "y", "x", "c")
SIZES = (2, 4, 4, 4, 2)
ZERO = AXES[1:]
TOKENS = 256


def places():
    for r in range(2):
        for zl in range(4):
            for y in range(4):
                for x in range(4):
                    for c in range(2):
                        yield r, zl, y, x, c


def rank(r, zl, y, x, c):
    return (((r * 4 + zl) * 4 + y) * 4 + x) * 2 + c


def send(value, target):
    pairs = [(rank(*place), rank(*target(*place))) for place in places()]
    return lax.ppermute(value, AXES, pairs)


def swap_cores(value):
    return send(value, lambda r, zl, y, x, c: (r, zl, y, x, 1 - c))


def swap_reps(value):
    return send(value, lambda r, zl, y, x, c: (1 - r, zl, y, x, c))


def along_line(value, k):
    return send(value, lambda r, zl, y, x, c: (r, zl ^ k, y, x, c))


def first_turn(value, k):
    return send(
        value,
        lambda r, zl, y, x, c: (r, zl, y, x ^ k, c) if c else (r, zl, y ^ k, x, c),
    )


def second_turn(value, k):
    return send(
        value,
        lambda r, zl, y, x, c: (r, zl, y ^ k, x, c) if c else (r, zl, y, x ^ k, c),
    )


def to_parity(value, j, other_rep):
    def target(r, zl, y, x, c):
        return r ^ other_rep, zl ^ (2 * j + c), y, x, zl % 2

    return send(value, target)


def turned(turn, values):
    got = {k: turn(values[k], k) for k in (1, 3, 2)}
    return [values[0]] + [got[k] for k in (1, 2, 3)]


def column(where, core, k3, k2, z):
    y = where[1] ^ jnp.where(core == 0, k2, k3)
    x = where[2] ^ jnp.where(core == 0, k3, k2)
    return pl.multiple_of(((z * 4 + y) * 4 + x) * 128, 128)


def precondition(where, p0, p1, p2, p3, low, high, pre):
    total = jnp.zeros((128, 128), jnp.float32)
    none = jnp.zeros((64, 128), jnp.bfloat16)
    for k3, piece in enumerate((p0, p1, p2, p3)):
        for k2 in range(4):
            at = [
                pl.ds(column(where, where[3], k3, k2, where[0] ^ kz), 128)
                for kz in range(4)
            ]
            rows = jnp.concatenate(
                [
                    jnp.concatenate([side[:, part] for part in at], axis=1)
                    for side in (low, high)
                ],
                axis=0,
            )
            held = []
            for kz in range(4):
                block = piece[k2, kz]
                held.append(jnp.where(where[3] == 0, block, none))
                held.append(jnp.where(where[3] == 0, none, block))
            total += jnp.dot(
                rows,
                jnp.concatenate(held, axis=0),
                preferred_element_type=jnp.float32,
            )
    pre[...] = total


def tiles(g, plane, *made):
    x = plane[...].reshape(1024, 256)
    for k, e in enumerate(made):
        part = lax.dot_general(
            g[k ^ (k >> 1)],
            x,
            (((1,), (1,)), ((), ())),
            preferred_element_type=jnp.float32,
        )
        e[...] = (part * (1.0 / TOKENS)).astype(e.dtype)


FIRST = 1


def assemble(where, *refs):
    pieces, (out, wide, sems) = refs[:8], refs[8:]
    core = where[3]
    places = []
    for side in range(2):
        held_by = core if side == 0 else 1 - core
        for k3 in range(4):
            for k2 in range(4):
                for j in range(2):
                    z = where[0] ^ (2 * j + lax.rem(where[0] + held_by, 2))
                    at = column(where, held_by, k3, k2, z)
                    places.append((pieces[side * 4 + k3], (k2 * 2 + j) * 128, at))
    copies = []
    for i in range(4):
        rows = slice(i * 16, i * 16 + 16)
        for piece, b, at in places:
            wide[rows, pl.ds(at, 128)] = piece[rows, b : b + 128].astype(jnp.float32)
        copies.append(pltpu.make_async_copy(wide.at[rows], out.at[rows], sems.at[i]))
        copies[-1].start()
    for copy in copies:
        copy.wait()


VMEM = pl.BlockSpec(memory_space=pltpu.VMEM)
SMEM = pl.BlockSpec(memory_space=pltpu.SMEM)
PARAMS = pltpu.CompilerParams(vmem_limit_bytes=12 * 1024 * 1024)


def call(body, name, shapes, ins):
    return pl.pallas_call(
        body,
        out_shape=shapes,
        in_specs=ins,
        out_specs=jax.tree.map(lambda _: VMEM, shapes),
        compiler_params=PARAMS,
        name=name,
    )


def on_device(acts, grads_out, act_inverse, grad_inverse):
    bf16, f32 = jnp.bfloat16, jnp.float32
    shape = jax.ShapeDtypeStruct
    c = lax.axis_index("c")
    where = jnp.stack(
        [lax.axis_index("zl"), lax.axis_index("y"), lax.axis_index("x"), c]
    ).astype(jnp.int32)
    first = c == 0

    block = jnp.stack([acts.T, grads_out.T])
    line = jnp.stack(turned(along_line, [block] * 4))
    held = turned(first_turn, [line] * 4)
    act_plane = jnp.stack([part[:, 0] for part in held])
    grad_plane = jnp.stack([part[:, 1] for part in held])

    def factor(rows):
        theirs = swap_cores(rows)
        return jnp.where(first, rows, theirs), jnp.where(first, theirs, rows)

    def partial(pieces, rows):
        return call(
            precondition, "precondition", shape((128, 128), f32), [SMEM] + [VMEM] * 6
        )(where, *pieces, *rows)

    act_rows, grad_rows = factor(act_inverse), factor(grad_inverse)
    part = partial(turned(second_turn, [act_plane] * 4), act_rows)
    part, grad_plane = lax.optimization_barrier((part, grad_plane))
    act = (part + swap_cores(part)).astype(bf16)
    part = partial(turned(second_turn, [grad_plane] * 4), grad_rows)
    grad = (part + swap_cores(part)).astype(bf16)

    here = [to_parity(act, j, 0) for j in (0, 1)]
    there = [to_parity(act, j, 1) for j in (0, 1)]
    pair = jnp.stack([jnp.concatenate(p, axis=1) for p in zip(here, there)])
    grad = jnp.concatenate([grad, swap_reps(grad)], axis=1)

    grads = jnp.stack([grad, second_turn(grad, 1)])
    plane = jnp.stack(turned(first_turn, [pair] * 4))
    grads = jnp.concatenate([grads, second_turn(grads, 3)], axis=0)
    made = call(tiles, "tiles", [shape((128, 1024), bf16)] * 4, [VMEM] * 2)(
        grads, plane
    )
    whole = turned(second_turn, made)
    own = [jnp.where(first, e[:64], e[64:]) for e in whole]
    give = [jnp.where(first, e[64:], e[:64]) for e in whole]
    one = swap_cores(jnp.stack([give[0], give[FIRST]]))
    sibling = {0: one[0], FIRST: one[1]}
    for k in (1, 2, 3):
        if k != FIRST:
            sibling[k] = swap_cores(give[k])
    return pl.pallas_call(
        assemble,
        out_shape=shape((64, 8192), f32),
        in_specs=[SMEM] + [VMEM] * 8,
        out_specs=pl.BlockSpec(memory_space=pltpu.HBM),
        scratch_shapes=[pltpu.VMEM((64, 8192), f32), pltpu.SemaphoreType.DMA((4,))],
        compiler_params=PARAMS,
        name="assemble",
    )(where, *own, *(sibling[k] for k in range(4)))


def solution(mesh):
    finer = Mesh(mesh.devices.reshape(SIZES), AXES)
    return jax.shard_map(
        on_device,
        mesh=finer,
        in_specs=(P("rep", ZERO), P("rep", ZERO), P(ZERO, None), P(ZERO, None)),
        out_specs=P(ZERO, None),
        check_vma=False,
    )
```

```python
import jax
import jax.numpy as jnp
from jax import lax
from jax.experimental import pallas as pl
from jax.experimental.pallas import tpu as pltpu
from jax.sharding import Mesh
from jax.sharding import PartitionSpec as P

AXES = ("rep", "zl", "y", "x", "c")
SIZES = (2, 4, 4, 4, 2)
ZERO = AXES[1:]
TOKENS = 256


def places():
    for r in range(2):
        for zl in range(4):
            for y in range(4):
                for x in range(4):
                    for c in range(2):
                        yield r, zl, y, x, c


def rank(r, zl, y, x, c):
    return (((r * 4 + zl) * 4 + y) * 4 + x) * 2 + c


def send(value, target):
    pairs = [(rank(*place), rank(*target(*place))) for place in places()]
    return lax.ppermute(value, AXES, pairs)


def swap_cores(value):
    return send(value, lambda r, zl, y, x, c: (r, zl, y, x, 1 - c))


def swap_reps(value):
    return send(value, lambda r, zl, y, x, c: (1 - r, zl, y, x, c))


def along_line(value, k):
    return send(value, lambda r, zl, y, x, c: (r, zl ^ k, y, x, c))


def first_turn(value, k):
    return send(
        value,
        lambda r, zl, y, x, c: (r, zl, y, x ^ k, c) if c else (r, zl, y ^ k, x, c),
    )


def second_turn(value, k):
    return send(
        value,
        lambda r, zl, y, x, c: (r, zl, y ^ k, x, c) if c else (r, zl, y, x ^ k, c),
    )


def to_parity(value, j, other_rep):
    def target(r, zl, y, x, c):
        return r ^ other_rep, zl ^ (2 * j + c), y, x, zl % 2

    return send(value, target)


def turned(turn, values):
    got = {k: turn(values[k], k) for k in (1, 3, 2)}
    return [values[0]] + [got[k] for k in (1, 2, 3)]


def column(where, core, k3, k2, z):
    y = where[1] ^ jnp.where(core == 0, k2, k3)
    x = where[2] ^ jnp.where(core == 0, k3, k2)
    return pl.multiple_of(((z * 4 + y) * 4 + x) * 128, 128)


def precondition(where, p0, p1, p2, p3, low, high, pre):
    total = jnp.zeros((128, 128), jnp.float32)
    none = jnp.zeros((64, 128), jnp.bfloat16)
    for k3, piece in enumerate((p0, p1, p2, p3)):
        for k2 in range(4):
            at = [
                pl.ds(column(where, where[3], k3, k2, where[0] ^ kz), 128)
                for kz in range(4)
            ]
            rows = jnp.concatenate(
                [
                    jnp.concatenate([side[:, part] for part in at], axis=1)
                    for side in (low, high)
                ],
                axis=0,
            )
            held = []
            for kz in range(4):
                block = piece[k2, kz]
                held.append(jnp.where(where[3] == 0, block, none))
                held.append(jnp.where(where[3] == 0, none, block))
            total += jnp.dot(
                rows,
                jnp.concatenate(held, axis=0),
                preferred_element_type=jnp.float32,
            )
    pre[...] = total


def tile(where, g, piece, keep, give):
    part = lax.dot_general(
        g[...],
        piece[...].reshape(1024, 256),
        (((1,), (1,)), ((), ())),
        preferred_element_type=jnp.float32,
    ) * (1.0 / TOKENS)
    low, high = part[:64], part[64:]
    keep[...] = jnp.where(where[3] == 0, low, high)
    give[...] = jnp.where(where[3] == 0, high, low)


def assemble(where, *refs):
    pieces, (out, wide, sems) = refs[:8], refs[8:]
    core = where[3]
    places = []
    for side in range(2):
        held_by = core if side == 0 else 1 - core
        for k3 in range(4):
            for k2 in range(4):
                for j in range(2):
                    z = where[0] ^ (2 * j + lax.rem(where[0] + held_by, 2))
                    at = column(where, held_by, k3, k2, z)
                    places.append((pieces[side * 4 + k3], (k2 * 2 + j) * 128, at))
    copies = []
    for i in range(4):
        rows = slice(i * 16, i * 16 + 16)
        for piece, b, at in places:
            wide[rows, pl.ds(at, 128)] = piece[rows, b : b + 128]
        copies.append(pltpu.make_async_copy(wide.at[rows], out.at[rows], sems.at[i]))
        copies[-1].start()
    for copy in copies:
        copy.wait()


VMEM = pl.BlockSpec(memory_space=pltpu.VMEM)
SMEM = pl.BlockSpec(memory_space=pltpu.SMEM)
PARAMS = pltpu.CompilerParams(vmem_limit_bytes=12 * 1024 * 1024)


def call(body, name, shapes, ins):
    return pl.pallas_call(
        body,
        out_shape=shapes,
        in_specs=ins,
        out_specs=jax.tree.map(lambda _: VMEM, shapes),
        compiler_params=PARAMS,
        name=name,
    )


def on_device(acts, grads_out, act_inverse, grad_inverse):
    bf16, f32 = jnp.bfloat16, jnp.float32
    shape = jax.ShapeDtypeStruct
    c = lax.axis_index("c")
    where = jnp.stack(
        [lax.axis_index("zl"), lax.axis_index("y"), lax.axis_index("x"), c]
    ).astype(jnp.int32)
    first = c == 0

    block = jnp.stack([acts.T, grads_out.T])
    line = jnp.stack(turned(along_line, [block] * 4))
    held = turned(first_turn, [line] * 4)
    act_plane = jnp.stack([part[:, 0] for part in held])
    grad_plane = jnp.stack([part[:, 1] for part in held])

    def factor(rows):
        theirs = swap_cores(rows)
        return jnp.where(first, rows, theirs), jnp.where(first, theirs, rows)

    def partial(pieces, rows):
        return call(
            precondition, "precondition", shape((128, 128), f32), [SMEM] + [VMEM] * 6
        )(where, *pieces, *rows)

    act_rows, grad_rows = factor(act_inverse), factor(grad_inverse)
    part = partial(turned(second_turn, [act_plane] * 4), act_rows)
    part, grad_plane = lax.optimization_barrier((part, grad_plane))
    act = (part + swap_cores(part)).astype(bf16)
    grad_pieces = turned(second_turn, [grad_plane] * 4)

    here = [to_parity(act, j, 0) for j in (0, 1)]
    there = [to_parity(act, j, 1) for j in (0, 1)]
    pair = jnp.stack([jnp.concatenate(p, axis=1) for p in zip(here, there)])
    pair, *grad_pieces = lax.optimization_barrier((pair, *grad_pieces))
    part = partial(grad_pieces, grad_rows)
    grad = (part + swap_cores(part)).astype(bf16)
    grad = jnp.concatenate([grad, swap_reps(grad)], axis=1)

    plane = jnp.stack(turned(first_turn, [pair] * 4))
    made = [
        call(tile, "tile", [shape((64, 1024), f32)] * 2, [SMEM, VMEM, VMEM])(
            where, grad, piece
        )
        for piece in turned(second_turn, [plane] * 4)
    ]
    own = [keep for keep, _ in made]
    sibling = [swap_cores(give) for _, give in made]
    return pl.pallas_call(
        assemble,
        out_shape=shape((64, 8192), f32),
        in_specs=[SMEM] + [VMEM] * 8,
        out_specs=pl.BlockSpec(memory_space=pltpu.HBM),
        scratch_shapes=[pltpu.VMEM((64, 8192), f32), pltpu.SemaphoreType.DMA((4,))],
        compiler_params=PARAMS,
        name="assemble",
    )(where, *own, *sibling)


def solution(mesh):
    finer = Mesh(mesh.devices.reshape(SIZES), AXES)
    return jax.shard_map(
        on_device,
        mesh=finer,
        in_specs=(P("rep", ZERO), P("rep", ZERO), P(ZERO, None), P(ZERO, None)),
        out_specs=P(ZERO, None),
        check_vma=False,
    )
```

```python
import jax
import jax.numpy as jnp
from jax import lax
from jax.experimental import pallas as pl
from jax.experimental.pallas import tpu as pltpu
from jax.sharding import Mesh
from jax.sharding import PartitionSpec as P

AXES = ("rep", "zl", "y", "x", "c")
SIZES = (2, 4, 4, 4, 2)
ZERO = AXES[1:]
TOKENS = 256


def places():
    for r in range(2):
        for zl in range(4):
            for y in range(4):
                for x in range(4):
                    for c in range(2):
                        yield r, zl, y, x, c


def rank(r, zl, y, x, c):
    return (((r * 4 + zl) * 4 + y) * 4 + x) * 2 + c


def send(value, target):
    pairs = [(rank(*place), rank(*target(*place))) for place in places()]
    return lax.ppermute(value, AXES, pairs)


def swap_cores(value):
    return send(value, lambda r, zl, y, x, c: (r, zl, y, x, 1 - c))


def swap_reps(value):
    return send(value, lambda r, zl, y, x, c: (1 - r, zl, y, x, c))


def along_line(value, k):
    return send(value, lambda r, zl, y, x, c: (r, zl ^ k, y, x, c))


def first_turn(value, k):
    return send(
        value,
        lambda r, zl, y, x, c: (r, zl, y, x ^ k, c) if c else (r, zl, y ^ k, x, c),
    )


def second_turn(value, k):
    return send(
        value,
        lambda r, zl, y, x, c: (r, zl, y ^ k, x, c) if c else (r, zl, y, x ^ k, c),
    )


def to_parity(value, j, other_rep):
    def target(r, zl, y, x, c):
        return r ^ other_rep, zl ^ (2 * j + c), y, x, zl % 2

    return send(value, target)


def turned(turn, values):
    got = {k: turn(values[k], k) for k in (1, 3, 2)}
    return [values[0]] + [got[k] for k in (1, 2, 3)]


def column(where, core, k3, k2, z):
    y = where[1] ^ jnp.where(core == 0, k2, k3)
    x = where[2] ^ jnp.where(core == 0, k3, k2)
    return pl.multiple_of(((z * 4 + y) * 4 + x) * 128, 128)


def precondition(where, p0, p1, p2, p3, low, high, pre):
    total = jnp.zeros((128, 128), jnp.float32)
    none = jnp.zeros((64, 128), jnp.bfloat16)
    for k3, piece in enumerate((p0, p1, p2, p3)):
        for k2 in range(4):
            at = [
                pl.ds(column(where, where[3], k3, k2, where[0] ^ kz), 128)
                for kz in range(4)
            ]
            rows = jnp.concatenate(
                [
                    jnp.concatenate([side[:, part] for part in at], axis=1)
                    for side in (low, high)
                ],
                axis=0,
            )
            held = []
            for kz in range(4):
                block = piece[k2, kz]
                held.append(jnp.where(where[3] == 0, block, none))
                held.append(jnp.where(where[3] == 0, none, block))
            total += jnp.dot(
                rows,
                jnp.concatenate(held, axis=0),
                preferred_element_type=jnp.float32,
            )
    pre[...] = total


def tile(where, g, piece, keep, give):
    part = lax.dot_general(
        g[...],
        piece[...].reshape(1024, 256),
        (((1,), (1,)), ((), ())),
        preferred_element_type=jnp.float32,
    ) * (1.0 / TOKENS)
    low, high = part[:64], part[64:]
    keep[...] = jnp.where(where[3] == 0, low, high)
    give[...] = jnp.where(where[3] == 0, high, low)


def assemble(where, *refs):
    pieces, (out, wide, sems) = refs[:8], refs[8:]
    core = where[3]
    places = []
    for side in range(2):
        held_by = core if side == 0 else 1 - core
        for k3 in range(4):
            for k2 in range(4):
                for j in range(2):
                    z = where[0] ^ (2 * j + lax.rem(where[0] + held_by, 2))
                    at = column(where, held_by, k3, k2, z)
                    places.append((pieces[side * 4 + k3], (k2 * 2 + j) * 128, at))
    copies = []
    for i in range(4):
        rows = slice(i * 16, i * 16 + 16)
        for piece, b, at in places:
            wide[rows, pl.ds(at, 128)] = piece[rows, b : b + 128]
        copies.append(pltpu.make_async_copy(wide.at[rows], out.at[rows], sems.at[i]))
        copies[-1].start()
    for copy in copies:
        copy.wait()


VMEM = pl.BlockSpec(memory_space=pltpu.VMEM)
SMEM = pl.BlockSpec(memory_space=pltpu.SMEM)
PARAMS = pltpu.CompilerParams(vmem_limit_bytes=12 * 1024 * 1024)


def call(body, name, shapes, ins):
    return pl.pallas_call(
        body,
        out_shape=shapes,
        in_specs=ins,
        out_specs=jax.tree.map(lambda _: VMEM, shapes),
        compiler_params=PARAMS,
        name=name,
    )


def on_device(acts, grads_out, act_inverse, grad_inverse):
    bf16, f32 = jnp.bfloat16, jnp.float32
    shape = jax.ShapeDtypeStruct
    c = lax.axis_index("c")
    where = jnp.stack(
        [lax.axis_index("zl"), lax.axis_index("y"), lax.axis_index("x"), c]
    ).astype(jnp.int32)
    first = c == 0

    block = jnp.stack([acts.T, grads_out.T])
    line = jnp.stack(turned(along_line, [block] * 4))
    held = turned(first_turn, [line] * 4)
    act_plane = jnp.stack([part[:, 0] for part in held])
    grad_plane = jnp.stack([part[:, 1] for part in held])

    def factor(rows):
        theirs = swap_cores(rows)
        return jnp.where(first, rows, theirs), jnp.where(first, theirs, rows)

    def partial(pieces, rows):
        return call(
            precondition, "precondition", shape((128, 128), f32), [SMEM] + [VMEM] * 6
        )(where, *pieces, *rows)

    act_rows, grad_rows = factor(act_inverse), factor(grad_inverse)
    part = partial(turned(second_turn, [act_plane] * 4), act_rows)
    part, grad_plane = lax.optimization_barrier((part, grad_plane))
    act = (part + swap_cores(part)).astype(bf16)
    grad_pieces = turned(second_turn, [grad_plane] * 4)

    here = [to_parity(act, j, 0) for j in (0, 1)]
    there = [to_parity(act, j, 1) for j in (0, 1)]
    pair = jnp.stack([jnp.concatenate(p, axis=1) for p in zip(here, there)])
    part = partial(grad_pieces, grad_rows)
    pair, part = lax.optimization_barrier((pair, part))
    grad = (part + swap_cores(part)).astype(bf16)
    plane = jnp.stack(turned(first_turn, [pair] * 4))
    plane, grad = lax.optimization_barrier((plane, grad))
    grad = jnp.concatenate([grad, swap_reps(grad)], axis=1)

    made = [
        call(tile, "tile", [shape((64, 1024), f32)] * 2, [SMEM, VMEM, VMEM])(
            where, grad, piece
        )
        for piece in turned(second_turn, [plane] * 4)
    ]
    own = [keep for keep, _ in made]
    sibling = [swap_cores(give) for _, give in made]
    return pl.pallas_call(
        assemble,
        out_shape=shape((64, 8192), f32),
        in_specs=[SMEM] + [VMEM] * 8,
        out_specs=pl.BlockSpec(memory_space=pltpu.HBM),
        scratch_shapes=[pltpu.VMEM((64, 8192), f32), pltpu.SemaphoreType.DMA((4,))],
        compiler_params=PARAMS,
        name="assemble",
    )(where, *own, *sibling)


def solution(mesh):
    finer = Mesh(mesh.devices.reshape(SIZES), AXES)
    return jax.shard_map(
        on_device,
        mesh=finer,
        in_specs=(P("rep", ZERO), P("rep", ZERO), P(ZERO, None), P(ZERO, None)),
        out_specs=P(ZERO, None),
        check_vma=False,
    )
```

```python
import functools

import jax
import jax.numpy as jnp
from jax import lax
from jax.experimental import pallas as pl
from jax.experimental.pallas import tpu as pltpu
from jax.sharding import Mesh
from jax.sharding import PartitionSpec as P

AXES = ("rep", "zl", "y", "x", "c")
SIZES = (2, 4, 4, 4, 2)
ZERO = AXES[1:]
TOKENS = 256


def places():
    for r in range(2):
        for zl in range(4):
            for y in range(4):
                for x in range(4):
                    for c in range(2):
                        yield r, zl, y, x, c


def rank(r, zl, y, x, c):
    return (((r * 4 + zl) * 4 + y) * 4 + x) * 2 + c


def send(value, target):
    pairs = [(rank(*place), rank(*target(*place))) for place in places()]
    return lax.ppermute(value, AXES, pairs)


def swap_cores(value):
    return send(value, lambda r, zl, y, x, c: (r, zl, y, x, 1 - c))


def swap_reps(value):
    return send(value, lambda r, zl, y, x, c: (1 - r, zl, y, x, c))


def along_line(value, k):
    return send(value, lambda r, zl, y, x, c: (r, zl ^ k, y, x, c))


def first_turn(value, k):
    return send(
        value,
        lambda r, zl, y, x, c: (r, zl, y, x ^ k, c) if c else (r, zl, y ^ k, x, c),
    )


def second_turn(value, k):
    return send(
        value,
        lambda r, zl, y, x, c: (r, zl, y ^ k, x, c) if c else (r, zl, y, x ^ k, c),
    )


def to_parity(value, j, other_rep):
    def target(r, zl, y, x, c):
        return r ^ other_rep, zl ^ (2 * j + c), y, x, zl % 2

    return send(value, target)


def turned(turn, values):
    got = {k: turn(values[k], k) for k in (1, 3, 2)}
    return [values[0]] + [got[k] for k in (1, 2, 3)]


def column(where, core, k3, k2, z):
    y = where[1] ^ jnp.where(core == 0, k2, k3)
    x = where[2] ^ jnp.where(core == 0, k3, k2)
    return pl.multiple_of(((z * 4 + y) * 4 + x) * 128, 128)


def precondition(flip, where, p0, p1, p2, p3, low, high, pre):
    total = jnp.zeros((128, 128), jnp.float32)
    none = jnp.zeros((64, 128), jnp.bfloat16)
    for k3, piece in enumerate((p0, p1, p2, p3)):
        for k2 in range(4):
            at = [
                pl.ds(column(where, where[3], k3, k2, where[0] ^ kz), 128)
                for kz in range(4)
            ]
            rows = jnp.concatenate(
                [
                    jnp.concatenate([side[:, part] for part in at], axis=1)
                    for side in (low, high)
                ],
                axis=0,
            )
            held = []
            for kz in range(4):
                block = piece[k2, kz]
                held.append(jnp.where(where[3] == 0, block, none))
                held.append(jnp.where(where[3] == 0, none, block))
            total += jnp.dot(
                rows,
                jnp.concatenate(held, axis=0),
                preferred_element_type=jnp.float32,
            )
    pre[...] = total.T if flip else total


def tile(where, g, piece, keep, give):
    blocks = [piece[k2, j] for k2 in range(4) for j in range(2)]
    part = jnp.dot(
        g[...],
        jnp.concatenate(blocks, axis=1),
        preferred_element_type=jnp.float32,
    ) * (1.0 / TOKENS)
    low, high = part[:64], part[64:]
    keep[...] = jnp.where(where[3] == 0, low, high)
    give[...] = jnp.where(where[3] == 0, high, low)


def assemble(where, *refs):
    pieces, (out, wide, sems) = refs[:8], refs[8:]
    core = where[3]
    places = []
    for side in range(2):
        held_by = core if side == 0 else 1 - core
        for k3 in range(4):
            for k2 in range(4):
                for j in range(2):
                    z = where[0] ^ (2 * j + lax.rem(where[0] + held_by, 2))
                    at = column(where, held_by, k3, k2, z)
                    places.append((pieces[side * 4 + k3], (k2 * 2 + j) * 128, at))
    copies = []
    for i in range(4):
        rows = slice(i * 16, i * 16 + 16)
        for piece, b, at in places:
            wide[rows, pl.ds(at, 128)] = piece[rows, b : b + 128]
        copies.append(pltpu.make_async_copy(wide.at[rows], out.at[rows], sems.at[i]))
        copies[-1].start()
    for copy in copies:
        copy.wait()


VMEM = pl.BlockSpec(memory_space=pltpu.VMEM)
SMEM = pl.BlockSpec(memory_space=pltpu.SMEM)
PARAMS = pltpu.CompilerParams(vmem_limit_bytes=12 * 1024 * 1024)


def call(body, name, shapes, ins):
    return pl.pallas_call(
        body,
        out_shape=shapes,
        in_specs=ins,
        out_specs=jax.tree.map(lambda _: VMEM, shapes),
        compiler_params=PARAMS,
        name=name,
    )


def on_device(acts, grads_out, act_inverse, grad_inverse):
    bf16, f32 = jnp.bfloat16, jnp.float32
    shape = jax.ShapeDtypeStruct
    c = lax.axis_index("c")
    where = jnp.stack(
        [lax.axis_index("zl"), lax.axis_index("y"), lax.axis_index("x"), c]
    ).astype(jnp.int32)
    first = c == 0

    block = jnp.stack([acts.T, grads_out.T])
    line = jnp.stack(turned(along_line, [block] * 4))
    held = turned(first_turn, [line] * 4)
    act_plane = jnp.stack([part[:, 0] for part in held])
    grad_plane = jnp.stack([part[:, 1] for part in held])

    def factor(rows):
        theirs = swap_cores(rows)
        return jnp.where(first, rows, theirs), jnp.where(first, theirs, rows)

    def partial(pieces, rows, flip):
        return call(
            functools.partial(precondition, flip),
            "precondition",
            shape((128, 128), f32),
            [SMEM] + [VMEM] * 6,
        )(where, *pieces, *rows)

    act_rows, grad_rows = factor(act_inverse), factor(grad_inverse)
    part = partial(turned(second_turn, [act_plane] * 4), act_rows, True)
    part, grad_plane = lax.optimization_barrier((part, grad_plane))
    act = (part + swap_cores(part)).astype(bf16)
    half = jnp.stack([grad_plane, second_turn(grad_plane, 1)])
    rest = second_turn(half, 3)
    grad_pieces = half[0], half[1], rest[1], rest[0]

    here = [to_parity(act, j, 0) for j in (0, 1)]
    there = [to_parity(act, j, 1) for j in (0, 1)]
    pair = jnp.stack([jnp.concatenate(p, axis=0) for p in zip(here, there)])
    part = partial(grad_pieces, grad_rows, False)
    pair, part = lax.optimization_barrier((pair, part))
    grad = (part + swap_cores(part)).astype(bf16)
    plane = jnp.stack(turned(first_turn, [pair] * 4))
    plane, grad = lax.optimization_barrier((plane, grad))
    grad = jnp.concatenate([grad, swap_reps(grad)], axis=1)

    made = [
        call(tile, "tile", [shape((64, 1024), f32)] * 2, [SMEM, VMEM, VMEM])(
            where, grad, piece
        )
        for piece in turned(second_turn, [plane] * 4)
    ]
    own = [keep for keep, _ in made]
    sibling = [swap_cores(give) for _, give in made]
    return pl.pallas_call(
        assemble,
        out_shape=shape((64, 8192), f32),
        in_specs=[SMEM] + [VMEM] * 8,
        out_specs=pl.BlockSpec(memory_space=pltpu.HBM),
        scratch_shapes=[pltpu.VMEM((64, 8192), f32), pltpu.SemaphoreType.DMA((4,))],
        compiler_params=PARAMS,
        name="assemble",
    )(where, *own, *sibling)


def solution(mesh):
    finer = Mesh(mesh.devices.reshape(SIZES), AXES)
    return jax.shard_map(
        on_device,
        mesh=finer,
        in_specs=(P("rep", ZERO), P("rep", ZERO), P(ZERO, None), P(ZERO, None)),
        out_specs=P(ZERO, None),
        check_vma=False,
    )
```

```python
import functools

import jax
import jax.numpy as jnp
from jax import lax
from jax.experimental import pallas as pl
from jax.experimental.pallas import tpu as pltpu
from jax.sharding import Mesh
from jax.sharding import PartitionSpec as P

AXES = ("rep", "zl", "y", "x", "c")
SIZES = (2, 4, 4, 4, 2)
ZERO = AXES[1:]
TOKENS = 256


def places():
    for r in range(2):
        for zl in range(4):
            for y in range(4):
                for x in range(4):
                    for c in range(2):
                        yield r, zl, y, x, c


def rank(r, zl, y, x, c):
    return (((r * 4 + zl) * 4 + y) * 4 + x) * 2 + c


def send(value, target):
    pairs = [(rank(*place), rank(*target(*place))) for place in places()]
    return lax.ppermute(value, AXES, pairs)


def swap_cores(value):
    return send(value, lambda r, zl, y, x, c: (r, zl, y, x, 1 - c))


def swap_reps(value):
    return send(value, lambda r, zl, y, x, c: (1 - r, zl, y, x, c))


def along_line(value, k):
    return send(value, lambda r, zl, y, x, c: (r, zl ^ k, y, x, c))


def first_turn(value, k):
    return send(
        value,
        lambda r, zl, y, x, c: (r, zl, y, x ^ k, c) if c else (r, zl, y ^ k, x, c),
    )


def second_turn(value, k):
    return send(
        value,
        lambda r, zl, y, x, c: (r, zl, y ^ k, x, c) if c else (r, zl, y, x ^ k, c),
    )


def to_parity(value, j, other_rep):
    def target(r, zl, y, x, c):
        return r ^ other_rep, zl ^ (2 * j + c), y, x, zl % 2

    return send(value, target)


def turned(turn, values):
    got = {k: turn(values[k], k) for k in (1, 3, 2)}
    return [values[0]] + [got[k] for k in (1, 2, 3)]


def column(where, core, k3, k2, z):
    y = where[1] ^ jnp.where(core == 0, k2, k3)
    x = where[2] ^ jnp.where(core == 0, k3, k2)
    return pl.multiple_of(((z * 4 + y) * 4 + x) * 128, 128)


def precondition(turns, flip, where, *refs):
    pieces, (low, high), pre = refs[: len(turns)], refs[-3:-1], refs[-1]
    rest = refs[len(turns) : -3]
    total = rest[0][...] if rest else jnp.zeros((128, 128), jnp.float32)
    none = jnp.zeros((64, 128), jnp.bfloat16)
    for k3, piece in zip(turns, pieces):
        for k2 in range(4):
            at = [
                pl.ds(column(where, where[3], k3, k2, where[0] ^ kz), 128)
                for kz in range(4)
            ]
            rows = jnp.concatenate(
                [
                    jnp.concatenate([side[:, part] for part in at], axis=1)
                    for side in (low, high)
                ],
                axis=0,
            )
            held = []
            for kz in range(4):
                block = piece[k2, kz]
                held.append(jnp.where(where[3] == 0, block, none))
                held.append(jnp.where(where[3] == 0, none, block))
            total += jnp.dot(
                rows,
                jnp.concatenate(held, axis=0),
                preferred_element_type=jnp.float32,
            )
    pre[...] = total.T if flip else total


def tile(where, g, piece, keep, give):
    blocks = [piece[k2, j] for k2 in range(4) for j in range(2)]
    part = jnp.dot(
        g[...],
        jnp.concatenate(blocks, axis=1),
        preferred_element_type=jnp.float32,
    ) * (1.0 / TOKENS)
    low, high = part[:64], part[64:]
    keep[...] = jnp.where(where[3] == 0, low, high)
    give[...] = jnp.where(where[3] == 0, high, low)


def assemble(where, *refs):
    pieces, (out, wide, sems) = refs[:8], refs[8:]
    core = where[3]
    places = []
    for side in range(2):
        held_by = core if side == 0 else 1 - core
        for k3 in range(4):
            for k2 in range(4):
                for j in range(2):
                    z = where[0] ^ (2 * j + lax.rem(where[0] + held_by, 2))
                    at = column(where, held_by, k3, k2, z)
                    places.append((pieces[side * 4 + k3], (k2 * 2 + j) * 128, at))
    copies = []
    for i in range(4):
        rows = slice(i * 16, i * 16 + 16)
        for piece, b, at in places:
            wide[rows, pl.ds(at, 128)] = piece[rows, b : b + 128]
        copies.append(pltpu.make_async_copy(wide.at[rows], out.at[rows], sems.at[i]))
        copies[-1].start()
    for copy in copies:
        copy.wait()


VMEM = pl.BlockSpec(memory_space=pltpu.VMEM)
SMEM = pl.BlockSpec(memory_space=pltpu.SMEM)
PARAMS = pltpu.CompilerParams(vmem_limit_bytes=12 * 1024 * 1024)


def call(body, name, shapes, ins):
    return pl.pallas_call(
        body,
        out_shape=shapes,
        in_specs=ins,
        out_specs=jax.tree.map(lambda _: VMEM, shapes),
        compiler_params=PARAMS,
        name=name,
    )


def on_device(acts, grads_out, act_inverse, grad_inverse):
    bf16, f32 = jnp.bfloat16, jnp.float32
    shape = jax.ShapeDtypeStruct
    c = lax.axis_index("c")
    where = jnp.stack(
        [lax.axis_index("zl"), lax.axis_index("y"), lax.axis_index("x"), c]
    ).astype(jnp.int32)
    first = c == 0

    block = jnp.stack([acts.T, grads_out.T])
    line = jnp.stack(turned(along_line, [block] * 4))
    held = turned(first_turn, [line] * 4)
    act_plane = jnp.stack([part[:, 0] for part in held])
    grad_plane = jnp.stack([part[:, 1] for part in held])

    def factor(rows):
        theirs = swap_cores(rows)
        return jnp.where(first, rows, theirs), jnp.where(first, theirs, rows)

    def partial(turns, pieces, rest, rows, flip):
        ins = [pieces[k] for k in turns] + rest + list(rows)
        return call(
            functools.partial(precondition, turns, flip),
            "precondition",
            shape((128, 128), f32),
            [SMEM] + [VMEM] * len(ins),
        )(where, *ins)

    act_rows, grad_rows = factor(act_inverse), factor(grad_inverse)
    pieces = turned(second_turn, [act_plane] * 4)
    part = partial((0, 3, 2), pieces, [], act_rows, False)
    part = partial((1,), pieces, [part], act_rows, True)
    part, grad_plane = lax.optimization_barrier((part, grad_plane))
    act = (part + swap_cores(part)).astype(bf16)
    half = jnp.stack([grad_plane, second_turn(grad_plane, 1)])

    here = [to_parity(act, j, 0) for j in (0, 1)]
    there = [to_parity(act, j, 1) for j in (0, 1)]
    half, here[0] = lax.optimization_barrier((half, here[0]))
    rest = second_turn(half, 3)
    grad_pieces = half[0], half[1], rest[1], rest[0]
    pair = jnp.stack([jnp.concatenate(p, axis=0) for p in zip(here, there)])
    part = partial((0, 1, 2, 3), grad_pieces, [], grad_rows, False)
    grad = (part + swap_cores(part)).astype(bf16)
    plane = jnp.stack(turned(first_turn, [pair] * 4))
    plane, grad = lax.optimization_barrier((plane, grad))
    grad = jnp.concatenate([grad, swap_reps(grad)], axis=1)

    made = [
        call(tile, "tile", [shape((64, 1024), f32)] * 2, [SMEM, VMEM, VMEM])(
            where, grad, piece
        )
        for piece in turned(second_turn, [plane] * 4)
    ]
    own = [keep for keep, _ in made]
    sibling = [swap_cores(give) for _, give in made]
    return pl.pallas_call(
        assemble,
        out_shape=shape((64, 8192), f32),
        in_specs=[SMEM] + [VMEM] * 8,
        out_specs=pl.BlockSpec(memory_space=pltpu.HBM),
        scratch_shapes=[pltpu.VMEM((64, 8192), f32), pltpu.SemaphoreType.DMA((4,))],
        compiler_params=PARAMS,
        name="assemble",
    )(where, *own, *sibling)


def solution(mesh):
    finer = Mesh(mesh.devices.reshape(SIZES), AXES)
    return jax.shard_map(
        on_device,
        mesh=finer,
        in_specs=(P("rep", ZERO), P("rep", ZERO), P(ZERO, None), P(ZERO, None)),
        out_specs=P(ZERO, None),
        check_vma=False,
    )
```

```python
import functools

import jax
import jax.numpy as jnp
from jax import lax
from jax.experimental import pallas as pl
from jax.experimental.pallas import tpu as pltpu
from jax.sharding import Mesh
from jax.sharding import PartitionSpec as P

AXES = ("rep", "zl", "y", "x", "c")
SIZES = (2, 4, 4, 4, 2)
ZERO = AXES[1:]
TOKENS = 256


def places():
    for r in range(2):
        for zl in range(4):
            for y in range(4):
                for x in range(4):
                    for c in range(2):
                        yield r, zl, y, x, c


def rank(r, zl, y, x, c):
    return (((r * 4 + zl) * 4 + y) * 4 + x) * 2 + c


def send(value, target):
    pairs = [(rank(*place), rank(*target(*place))) for place in places()]
    return lax.ppermute(value, AXES, pairs)


def swap_cores(value):
    return send(value, lambda r, zl, y, x, c: (r, zl, y, x, 1 - c))


def swap_reps(value):
    return send(value, lambda r, zl, y, x, c: (1 - r, zl, y, x, c))


def along_line(value, k):
    return send(value, lambda r, zl, y, x, c: (r, zl ^ k, y, x, c))


def first_turn(value, k):
    return send(
        value,
        lambda r, zl, y, x, c: (r, zl, y, x ^ k, c) if c else (r, zl, y ^ k, x, c),
    )


def second_turn(value, k):
    return send(
        value,
        lambda r, zl, y, x, c: (r, zl, y ^ k, x, c) if c else (r, zl, y, x ^ k, c),
    )


def to_parity(value, j, other_rep):
    def target(r, zl, y, x, c):
        return r ^ other_rep, zl ^ (2 * j + c), y, x, zl % 2

    return send(value, target)


def turned(turn, values):
    got = {k: turn(values[k], k) for k in (1, 3, 2)}
    return [values[0]] + [got[k] for k in (1, 2, 3)]


def column(where, core, k3, k2, z):
    y = where[1] ^ jnp.where(core == 0, k2, k3)
    x = where[2] ^ jnp.where(core == 0, k3, k2)
    return pl.multiple_of(((z * 4 + y) * 4 + x) * 128, 128)


def precondition(turns, flip, where, *refs):
    pieces, (low, high), pre = refs[: len(turns)], refs[-3:-1], refs[-1]
    rest = refs[len(turns) : -3]
    total = rest[0][...] if rest else jnp.zeros((128, 128), jnp.float32)
    none = jnp.zeros((64, 128), jnp.bfloat16)
    for k3, piece in zip(turns, pieces):
        for k2 in range(4):
            at = [
                pl.ds(column(where, where[3], k3, k2, where[0] ^ kz), 128)
                for kz in range(4)
            ]
            rows = jnp.concatenate(
                [
                    jnp.concatenate([side[:, part] for part in at], axis=1)
                    for side in (low, high)
                ],
                axis=0,
            )
            held = []
            for kz in range(4):
                block = piece[k2, kz]
                held.append(jnp.where(where[3] == 0, block, none))
                held.append(jnp.where(where[3] == 0, none, block))
            total += jnp.dot(
                rows,
                jnp.concatenate(held, axis=0),
                preferred_element_type=jnp.float32,
            )
    pre[...] = total.T if flip else total


def tile(g, piece, keep, give):
    blocks = [piece[k2, j] for k2 in range(4) for j in range(2)]
    part = jnp.dot(
        g[...],
        jnp.concatenate(blocks, axis=1),
        preferred_element_type=jnp.float32,
    ) * (1.0 / TOKENS)
    keep[...] = part[:64]
    give[...] = part[64:]


def assemble(where, *refs):
    pieces, (out, wide, sems) = refs[:8], refs[8:]
    core = where[3]
    places = []
    for side in range(2):
        held_by = core if side == 0 else 1 - core
        for k3 in range(4):
            for k2 in range(4):
                for j in range(2):
                    z = where[0] ^ (2 * j + lax.rem(where[0] + held_by, 2))
                    at = column(where, held_by, k3, k2, z)
                    places.append((pieces[side * 4 + k3], (k2 * 2 + j) * 128, at))
    copies = []
    for i in range(4):
        rows = slice(i * 16, i * 16 + 16)
        for piece, b, at in places:
            wide[rows, pl.ds(at, 128)] = piece[rows, b : b + 128]
        copies.append(pltpu.make_async_copy(wide.at[rows], out.at[rows], sems.at[i]))
        copies[-1].start()
    for copy in copies:
        copy.wait()


VMEM = pl.BlockSpec(memory_space=pltpu.VMEM)
SMEM = pl.BlockSpec(memory_space=pltpu.SMEM)
PARAMS = pltpu.CompilerParams(vmem_limit_bytes=12 * 1024 * 1024)


def call(body, name, shapes, ins):
    return pl.pallas_call(
        body,
        out_shape=shapes,
        in_specs=ins,
        out_specs=jax.tree.map(lambda _: VMEM, shapes),
        compiler_params=PARAMS,
        name=name,
    )


def on_device(acts, grads_out, act_inverse, grad_inverse):
    bf16, f32 = jnp.bfloat16, jnp.float32
    shape = jax.ShapeDtypeStruct
    c = lax.axis_index("c")
    where = jnp.stack(
        [lax.axis_index("zl"), lax.axis_index("y"), lax.axis_index("x"), c]
    ).astype(jnp.int32)
    first = c == 0

    block = jnp.stack([acts.T, grads_out.T])
    line = jnp.stack(turned(along_line, [block] * 4))
    held = turned(first_turn, [line] * 4)
    act_plane = jnp.stack([part[:, 0] for part in held])
    grad_plane = jnp.stack([part[:, 1] for part in held])

    def factor(rows):
        theirs = swap_cores(rows)
        return jnp.where(first, rows, theirs), jnp.where(first, theirs, rows)

    def partial(turns, pieces, rest, rows, flip):
        ins = [pieces[k] for k in turns] + rest + list(rows)
        return call(
            functools.partial(precondition, turns, flip),
            "precondition",
            shape((128, 128), f32),
            [SMEM] + [VMEM] * len(ins),
        )(where, *ins)

    act_rows, grad_rows = factor(act_inverse), factor(grad_inverse)
    pieces = turned(second_turn, [act_plane] * 4)
    part = partial((0, 3, 2), pieces, [], act_rows, False)
    part = partial((1,), pieces, [part], act_rows, True)
    part, grad_plane = lax.optimization_barrier((part, grad_plane))
    act = (part + swap_cores(part)).astype(bf16)
    half = jnp.stack([grad_plane, second_turn(grad_plane, 1)])

    there = [to_parity(act, j, 1) for j in (0, 1)]
    here = [to_parity(act, j, 0) for j in (0, 1)]
    half, here[0] = lax.optimization_barrier((half, here[0]))
    rest = second_turn(half, 3)
    grad_pieces = half[0], half[1], rest[1], rest[0]
    pair = jnp.stack([*there, *here]).reshape(2, 2, 128, 128)
    pair = jnp.swapaxes(pair, 0, 1).reshape(2, 256, 128)
    part = partial((0, 1, 2, 3), grad_pieces, [], grad_rows, False)
    grad = (part + swap_cores(part)).astype(bf16)
    plane = jnp.stack(turned(first_turn, [pair] * 4))
    grad = jnp.where(first, grad, jnp.concatenate([grad[64:], grad[:64]], axis=0))
    plane, grad = lax.optimization_barrier((plane, grad))
    grad = jnp.concatenate([swap_reps(grad), grad], axis=1)

    made = [
        call(tile, "tile", [shape((64, 1024), f32)] * 2, [VMEM] * 2)(grad, piece)
        for piece in turned(second_turn, [plane] * 4)
    ]
    own = [keep for keep, _ in made]
    sibling = [swap_cores(give) for _, give in made]
    return pl.pallas_call(
        assemble,
        out_shape=shape((64, 8192), f32),
        in_specs=[SMEM] + [VMEM] * 8,
        out_specs=pl.BlockSpec(memory_space=pltpu.HBM),
        scratch_shapes=[pltpu.VMEM((64, 8192), f32), pltpu.SemaphoreType.DMA((4,))],
        compiler_params=PARAMS,
        name="assemble",
    )(where, *own, *sibling)


def solution(mesh):
    finer = Mesh(mesh.devices.reshape(SIZES), AXES)
    return jax.shard_map(
        on_device,
        mesh=finer,
        in_specs=(P("rep", ZERO), P("rep", ZERO), P(ZERO, None), P(ZERO, None)),
        out_specs=P(ZERO, None),
        check_vma=False,
    )
```

```python
import functools

import jax
import jax.numpy as jnp
from jax import lax
from jax.experimental import pallas as pl
from jax.experimental.pallas import tpu as pltpu
from jax.sharding import Mesh
from jax.sharding import PartitionSpec as P

AXES = ("rep", "zl", "y", "x", "c")
SIZES = (2, 4, 4, 4, 2)
ZERO = AXES[1:]
TOKENS = 256


def places():
    for r in range(2):
        for zl in range(4):
            for y in range(4):
                for x in range(4):
                    for c in range(2):
                        yield r, zl, y, x, c


def rank(r, zl, y, x, c):
    return (((r * 4 + zl) * 4 + y) * 4 + x) * 2 + c


def send(value, target):
    pairs = [(rank(*place), rank(*target(*place))) for place in places()]
    return lax.ppermute(value, AXES, pairs)


def swap_cores(value):
    return send(value, lambda r, zl, y, x, c: (r, zl, y, x, 1 - c))


def swap_reps(value):
    return send(value, lambda r, zl, y, x, c: (1 - r, zl, y, x, c))


def along_line(value, k):
    return send(value, lambda r, zl, y, x, c: (r, zl ^ k, y, x, c))


def first_turn(value, k):
    return send(
        value,
        lambda r, zl, y, x, c: (r, zl, y, x ^ k, c) if c else (r, zl, y ^ k, x, c),
    )


def second_turn(value, k):
    return send(
        value,
        lambda r, zl, y, x, c: (r, zl, y ^ k, x, c) if c else (r, zl, y, x ^ k, c),
    )


def to_parity(value, j, other_rep):
    def target(r, zl, y, x, c):
        return r ^ other_rep, zl ^ (2 * j + c), y, x, zl % 2

    return send(value, target)


def turned(turn, values):
    got = {k: turn(values[k], k) for k in (1, 3, 2)}
    return [values[0]] + [got[k] for k in (1, 2, 3)]


def here_is():
    return [lax.axis_index(name) for name in ("zl", "y", "x", "c")]


def column(where, core, k3, k2, z):
    y = where[1] ^ jnp.where(core == 0, k2, k3)
    x = where[2] ^ jnp.where(core == 0, k3, k2)
    return pl.multiple_of(((z * 4 + y) * 4 + x) * 128, 128)


def precondition(turns, flip, *refs):
    where = here_is()
    pieces, (low, high), pre = refs[: len(turns)], refs[-3:-1], refs[-1]
    rest = refs[len(turns) : -3]
    total = rest[0][...] if rest else jnp.zeros((128, 128), jnp.float32)
    none = jnp.zeros((64, 128), jnp.bfloat16)
    for k3, piece in zip(turns, pieces):
        for k2 in range(4):
            at = [
                pl.ds(column(where, where[3], k3, k2, where[0] ^ kz), 128)
                for kz in range(4)
            ]
            rows = jnp.concatenate(
                [
                    jnp.concatenate([side[:, part] for part in at], axis=1)
                    for side in (low, high)
                ],
                axis=0,
            )
            held = []
            for kz in range(4):
                block = piece[k2, kz]
                held.append(jnp.where(where[3] == 0, block, none))
                held.append(jnp.where(where[3] == 0, none, block))
            total += jnp.dot(
                rows,
                jnp.concatenate(held, axis=0),
                preferred_element_type=jnp.float32,
            )
    pre[...] = total.T if flip else total


def tile(g, piece, keep, give):
    blocks = [piece[k2, j] for k2 in range(4) for j in range(2)]
    part = jnp.dot(
        g[...],
        jnp.concatenate(blocks, axis=1),
        preferred_element_type=jnp.float32,
    ) * (1.0 / TOKENS)
    keep[...] = part[:64]
    give[...] = part[64:]


def assemble(*refs):
    where = here_is()
    pieces, (out, wide, sems) = refs[:8], refs[8:]
    core = where[3]
    places = []
    for side in range(2):
        held_by = core if side == 0 else 1 - core
        for k3 in range(4):
            for k2 in range(4):
                for j in range(2):
                    z = where[0] ^ (2 * j + lax.rem(where[0] + held_by, 2))
                    at = column(where, held_by, k3, k2, z)
                    places.append((pieces[side * 4 + k3], (k2 * 2 + j) * 128, at))
    copies = []
    for i in range(4):
        rows = slice(i * 16, i * 16 + 16)
        for piece, b, at in places:
            wide[rows, pl.ds(at, 128)] = piece[rows, b : b + 128]
        copies.append(pltpu.make_async_copy(wide.at[rows], out.at[rows], sems.at[i]))
        copies[-1].start()
    for copy in copies:
        copy.wait()


VMEM = pl.BlockSpec(memory_space=pltpu.VMEM)
PARAMS = pltpu.CompilerParams(vmem_limit_bytes=12 * 1024 * 1024)


def call(body, name, shapes, ins):
    return pl.pallas_call(
        body,
        out_shape=shapes,
        in_specs=ins,
        out_specs=jax.tree.map(lambda _: VMEM, shapes),
        compiler_params=PARAMS,
        name=name,
    )


def on_device(acts, grads_out, act_inverse, grad_inverse):
    bf16, f32 = jnp.bfloat16, jnp.float32
    shape = jax.ShapeDtypeStruct
    c = lax.axis_index("c")
    first = c == 0

    block = jnp.stack([acts.T, grads_out.T])
    line = jnp.stack(turned(along_line, [block] * 4))
    held = turned(first_turn, [line] * 4)
    act_plane = jnp.stack([part[:, 0] for part in held])
    grad_plane = jnp.stack([part[:, 1] for part in held])

    def factor(rows):
        theirs = swap_cores(rows)
        return jnp.where(first, rows, theirs), jnp.where(first, theirs, rows)

    def partial(turns, pieces, rest, rows, flip):
        ins = [pieces[k] for k in turns] + rest + list(rows)
        return call(
            functools.partial(precondition, turns, flip),
            "precondition",
            shape((128, 128), f32),
            [VMEM] * len(ins),
        )(*ins)

    act_rows, grad_rows = factor(act_inverse), factor(grad_inverse)
    pieces = turned(second_turn, [act_plane] * 4)
    part = partial((0, 3, 2), pieces, [], act_rows, False)
    part = partial((1,), pieces, [part], act_rows, True)
    part, grad_plane = lax.optimization_barrier((part, grad_plane))
    act = (part + swap_cores(part)).astype(bf16)
    half = jnp.stack([grad_plane, second_turn(grad_plane, 1)])

    there = [to_parity(act, j, 1) for j in (0, 1)]
    here = [to_parity(act, j, 0) for j in (0, 1)]
    half, here[0] = lax.optimization_barrier((half, here[0]))
    rest = second_turn(half, 3)
    grad_pieces = half[0], half[1], rest[1], rest[0]
    pair = jnp.stack([*there, *here]).reshape(2, 2, 128, 128)
    pair = jnp.swapaxes(pair, 0, 1).reshape(2, 256, 128)
    part = partial((0, 1, 2, 3), grad_pieces, [], grad_rows, False)
    plane = jnp.stack(turned(first_turn, [pair] * 4))
    grad = (part + swap_cores(part)).astype(bf16)
    grad = jnp.where(first, grad, jnp.concatenate([grad[64:], grad[:64]], axis=0))
    plane, grad = lax.optimization_barrier((plane, grad))
    grad = jnp.concatenate([swap_reps(grad), grad], axis=1)

    made = [
        call(tile, "tile", [shape((64, 1024), f32)] * 2, [VMEM] * 2)(grad, piece)
        for piece in turned(second_turn, [plane] * 4)
    ]
    own = [keep for keep, _ in made]
    sibling = [swap_cores(give) for _, give in made]
    return pl.pallas_call(
        assemble,
        out_shape=shape((64, 8192), f32),
        in_specs=[VMEM] * 8,
        out_specs=pl.BlockSpec(memory_space=pltpu.HBM),
        scratch_shapes=[pltpu.VMEM((64, 8192), f32), pltpu.SemaphoreType.DMA((4,))],
        compiler_params=PARAMS,
        name="assemble",
    )(*own, *sibling)


def solution(mesh):
    finer = Mesh(mesh.devices.reshape(SIZES), AXES)
    return jax.shard_map(
        on_device,
        mesh=finer,
        in_specs=(P("rep", ZERO), P("rep", ZERO), P(ZERO, None), P(ZERO, None)),
        out_specs=P(ZERO, None),
        check_vma=False,
    )
```

```python
import functools

import jax
import jax.numpy as jnp
from jax import lax
from jax.experimental import pallas as pl
from jax.experimental.pallas import tpu as pltpu
from jax.sharding import Mesh
from jax.sharding import PartitionSpec as P

AXES = ("rep", "zl", "y", "x", "c")
SIZES = (2, 4, 4, 4, 2)
ZERO = AXES[1:]
TOKENS = 256


def places():
    for r in range(2):
        for zl in range(4):
            for y in range(4):
                for x in range(4):
                    for c in range(2):
                        yield r, zl, y, x, c


def rank(r, zl, y, x, c):
    return (((r * 4 + zl) * 4 + y) * 4 + x) * 2 + c


def send(value, target):
    pairs = [(rank(*place), rank(*target(*place))) for place in places()]
    return lax.ppermute(value, AXES, pairs)


def swap_cores(value):
    return send(value, lambda r, zl, y, x, c: (r, zl, y, x, 1 - c))


def swap_reps(value):
    return send(value, lambda r, zl, y, x, c: (1 - r, zl, y, x, c))


def along_line(value, k):
    return send(value, lambda r, zl, y, x, c: (r, zl ^ k, y, x, c))


def first_turn(value, k):
    return send(
        value,
        lambda r, zl, y, x, c: (r, zl, y, x ^ k, c) if c else (r, zl, y ^ k, x, c),
    )


def second_turn(value, k):
    return send(
        value,
        lambda r, zl, y, x, c: (r, zl, y ^ k, x, c) if c else (r, zl, y, x ^ k, c),
    )


def stacked(turn, value, order):
    got = turned(turn, [value] * 4)
    return jnp.stack([got[k] for k in order])


def to_parity(value, j, other_rep):
    def target(r, zl, y, x, c):
        return r ^ other_rep, zl ^ (2 * j + c), y, x, zl % 2

    return send(value, target)


def turned(turn, values):
    got = {k: turn(values[k], k) for k in (1, 3, 2)}
    return [values[0]] + [got[k] for k in (1, 2, 3)]


ORDER_F = (0, 1, 3, 2)
ORDER_Z, ORDER_2, ORDER_B = (0, 2, 1, 3), (0, 2, 1, 3), (0, 2, 1, 3)


def here_is():
    return [lax.axis_index(name) for name in ("zl", "y", "x", "c")]


def column(where, core, k3, k2, z):
    y = where[1] ^ jnp.where(core == 0, k2, k3)
    x = where[2] ^ jnp.where(core == 0, k3, k2)
    return pl.multiple_of(((z * 4 + y) * 4 + x) * 128, 128)


def precondition(turns, flip, *refs):
    where = here_is()
    pieces, (low, high), pre = refs[: len(turns)], refs[-3:-1], refs[-1]
    rest = refs[len(turns) : -3]
    total = rest[0][...] if rest else jnp.zeros((128, 128), jnp.float32)
    none = jnp.zeros((64, 128), jnp.bfloat16)
    for k3, piece in zip(turns, pieces):
        for n, k2 in enumerate(ORDER_2):
            at = [
                pl.ds(column(where, where[3], k3, k2, where[0] ^ kz), 128)
                for kz in ORDER_Z
            ]
            rows = jnp.concatenate(
                [
                    jnp.concatenate([side[:, part] for part in at], axis=1)
                    for side in (low, high)
                ],
                axis=0,
            )
            held = []
            for m in range(4):
                block = piece[n, m]
                held.append(jnp.where(where[3] == 0, block, none))
                held.append(jnp.where(where[3] == 0, none, block))
            total += jnp.dot(
                rows,
                jnp.concatenate(held, axis=0),
                preferred_element_type=jnp.float32,
            )
    pre[...] = total.T if flip else total


def tile(g, piece, keep, give):
    blocks = [piece[k2, j] for k2 in range(4) for j in range(2)]
    part = jnp.dot(
        g[...],
        jnp.concatenate(blocks, axis=1),
        preferred_element_type=jnp.float32,
    ) * (1.0 / TOKENS)
    keep[...] = part[:64]
    give[...] = part[64:]


def assemble(*refs):
    where = here_is()
    pieces, (out, wide, sems) = refs[:8], refs[8:]
    core = where[3]
    places = []
    for side in range(2):
        held_by = core if side == 0 else 1 - core
        for m, k3 in enumerate(ORDER_F):
            for n, k2 in enumerate(ORDER_B):
                for j in range(2):
                    z = where[0] ^ (2 * j + lax.rem(where[0] + held_by, 2))
                    at = column(where, held_by, k3, k2, z)
                    places.append((pieces[side * 4 + m], (n * 2 + j) * 128, at))
    copies = []
    for i in range(4):
        rows = slice(i * 16, i * 16 + 16)
        for piece, b, at in places:
            wide[rows, pl.ds(at, 128)] = piece[rows, b : b + 128]
        copies.append(pltpu.make_async_copy(wide.at[rows], out.at[rows], sems.at[i]))
        copies[-1].start()
    for copy in copies:
        copy.wait()


VMEM = pl.BlockSpec(memory_space=pltpu.VMEM)
PARAMS = pltpu.CompilerParams(vmem_limit_bytes=12 * 1024 * 1024)


def call(body, name, shapes, ins):
    return pl.pallas_call(
        body,
        out_shape=shapes,
        in_specs=ins,
        out_specs=jax.tree.map(lambda _: VMEM, shapes),
        compiler_params=PARAMS,
        name=name,
    )


def on_device(acts, grads_out, act_inverse, grad_inverse):
    bf16, f32 = jnp.bfloat16, jnp.float32
    shape = jax.ShapeDtypeStruct
    c = lax.axis_index("c")
    first = c == 0

    block = jnp.stack([acts.T, grads_out.T])
    line = stacked(along_line, block, ORDER_Z)
    held = turned(first_turn, [line] * 4)
    held = [held[k] for k in ORDER_2]
    act_plane = jnp.stack([part[:, 0] for part in held])
    grad_plane = jnp.stack([part[:, 1] for part in held])

    def factor(rows):
        theirs = swap_cores(rows)
        return jnp.where(first, rows, theirs), jnp.where(first, theirs, rows)

    def partial(turns, pieces, rest, rows, flip):
        ins = [pieces[k] for k in turns] + rest + list(rows)
        return call(
            functools.partial(precondition, turns, flip),
            "precondition",
            shape((128, 128), f32),
            [VMEM] * len(ins),
        )(*ins)

    act_rows, grad_rows = factor(act_inverse), factor(grad_inverse)
    pieces = turned(second_turn, [act_plane] * 4)
    part = partial((0, 2, 3), pieces, [], act_rows, False)
    part = partial((1,), pieces, [part], act_rows, True)
    part, grad_plane = lax.optimization_barrier((part, grad_plane))
    act = (part + swap_cores(part)).astype(bf16)
    half = jnp.stack([grad_plane, second_turn(grad_plane, 1)])

    there = [to_parity(act, j, 1) for j in (0, 1)]
    here = [to_parity(act, j, 0) for j in (0, 1)]
    half, there[0] = lax.optimization_barrier((half, there[0]))
    rest = second_turn(half, 3)
    grad_pieces = half[0], half[1], rest[1], rest[0]
    pair = jnp.stack([*there, *here]).reshape(2, 2, 128, 128)
    pair = jnp.swapaxes(pair, 0, 1).reshape(2, 256, 128)
    part = partial((0, 1, 2, 3), grad_pieces, [], grad_rows, False)
    plane = stacked(first_turn, pair, ORDER_B)
    grad = (part + swap_cores(part)).astype(bf16)
    grad = jnp.where(first, grad, jnp.concatenate([grad[64:], grad[:64]], axis=0))
    plane, grad = lax.optimization_barrier((plane, grad))
    grad = jnp.concatenate([swap_reps(grad), grad], axis=1)

    made = [
        call(tile, "tile", [shape((64, 1024), f32)] * 2, [VMEM] * 2)(grad, piece)
        for piece in turned(second_turn, [plane] * 4)
    ]
    own = [made[k][0] for k in ORDER_F]
    sibling = [swap_cores(made[k][1]) for k in ORDER_F]
    return pl.pallas_call(
        assemble,
        out_shape=shape((64, 8192), f32),
        in_specs=[VMEM] * 8,
        out_specs=pl.BlockSpec(memory_space=pltpu.HBM),
        scratch_shapes=[pltpu.VMEM((64, 8192), f32), pltpu.SemaphoreType.DMA((4,))],
        compiler_params=PARAMS,
        name="assemble",
    )(*own, *sibling)


def solution(mesh):
    finer = Mesh(mesh.devices.reshape(SIZES), AXES)
    return jax.shard_map(
        on_device,
        mesh=finer,
        in_specs=(P("rep", ZERO), P("rep", ZERO), P(ZERO, None), P(ZERO, None)),
        out_specs=P(ZERO, None),
        check_vma=False,
    )
```

```python
import functools

import jax
import jax.numpy as jnp
from jax import lax
from jax.experimental import pallas as pl
from jax.experimental.pallas import tpu as pltpu
from jax.sharding import Mesh
from jax.sharding import PartitionSpec as P

AXES = ("rep", "zl", "y", "x", "c")
SIZES = (2, 4, 4, 4, 2)
ZERO = AXES[1:]
TOKENS = 256


def places():
    for r in range(2):
        for zl in range(4):
            for y in range(4):
                for x in range(4):
                    for c in range(2):
                        yield r, zl, y, x, c


def rank(r, zl, y, x, c):
    return (((r * 4 + zl) * 4 + y) * 4 + x) * 2 + c


def send(value, target):
    pairs = [(rank(*place), rank(*target(*place))) for place in places()]
    return lax.ppermute(value, AXES, pairs)


def swap_cores(value):
    return send(value, lambda r, zl, y, x, c: (r, zl, y, x, 1 - c))


def swap_reps(value):
    return send(value, lambda r, zl, y, x, c: (1 - r, zl, y, x, c))


def along_line(value, k):
    return send(value, lambda r, zl, y, x, c: (r, zl ^ k, y, x, c))


def first_turn(value, k):
    return send(
        value,
        lambda r, zl, y, x, c: (r, zl, y, x ^ k, c) if c else (r, zl, y ^ k, x, c),
    )


def second_turn(value, k):
    return send(
        value,
        lambda r, zl, y, x, c: (r, zl, y ^ k, x, c) if c else (r, zl, y, x ^ k, c),
    )


def stacked(turn, value, order):
    got = turned(turn, [value] * 4)
    return jnp.stack([got[k] for k in order])


def to_parity(value, j, other_rep):
    def target(r, zl, y, x, c):
        return r ^ other_rep, zl ^ (2 * j + c), y, x, zl % 2

    return send(value, target)


def turned(turn, values):
    got = {k: turn(values[k], k) for k in (1, 3, 2)}
    return [values[0]] + [got[k] for k in (1, 2, 3)]


ORDER_F = (0, 2, 1, 3)
ORDER_Z, ORDER_2, ORDER_B = (0, 1, 2, 3), (0, 1, 3, 2), (0, 1, 3, 2)


def here_is():
    return [lax.axis_index(name) for name in ("zl", "y", "x", "c")]


def column(where, core, k3, k2, z):
    y = where[1] ^ jnp.where(core == 0, k2, k3)
    x = where[2] ^ jnp.where(core == 0, k3, k2)
    return pl.multiple_of(((z * 4 + y) * 4 + x) * 128, 128)


def precondition(turns, flip, *refs):
    where = here_is()
    pieces, (low, high), pre = refs[: len(turns)], refs[-3:-1], refs[-1]
    rest = refs[len(turns) : -3]
    total = rest[0][...] if rest else jnp.zeros((128, 128), jnp.float32)
    none = jnp.zeros((64, 128), jnp.bfloat16)
    for k3, piece in zip(turns, pieces):
        for n, k2 in enumerate(ORDER_2):
            at = [
                pl.ds(column(where, where[3], k3, k2, where[0] ^ kz), 128)
                for kz in ORDER_Z
            ]
            rows = jnp.concatenate(
                [
                    jnp.concatenate([side[:, part] for part in at], axis=1)
                    for side in (low, high)
                ],
                axis=0,
            )
            held = []
            for m in range(4):
                block = piece[n, m]
                held.append(jnp.where(where[3] == 0, block, none))
                held.append(jnp.where(where[3] == 0, none, block))
            total += jnp.dot(
                rows,
                jnp.concatenate(held, axis=0),
                preferred_element_type=jnp.float32,
            )
    pre[...] = total.T if flip else total


def tile(g, piece, keep, give):
    blocks = [piece[k2, j] for k2 in range(4) for j in range(2)]
    part = jnp.dot(
        g[...],
        jnp.concatenate(blocks, axis=1),
        preferred_element_type=jnp.float32,
    ) * (1.0 / TOKENS)
    keep[...] = part[:64]
    give[...] = part[64:]


def assemble(*refs):
    where = here_is()
    pieces, (out, wide, sems) = refs[:8], refs[8:]
    core = where[3]
    places = []
    for side in range(2):
        held_by = core if side == 0 else 1 - core
        for m, k3 in enumerate(ORDER_F):
            for n, k2 in enumerate(ORDER_B):
                for j in range(2):
                    z = where[0] ^ (2 * j + lax.rem(where[0] + held_by, 2))
                    at = column(where, held_by, k3, k2, z)
                    places.append((pieces[side * 4 + m], (n * 2 + j) * 128, at))
    copies = []
    for i in range(4):
        rows = slice(i * 16, i * 16 + 16)
        for piece, b, at in places:
            wide[rows, pl.ds(at, 128)] = piece[rows, b : b + 128]
        copies.append(pltpu.make_async_copy(wide.at[rows], out.at[rows], sems.at[i]))
        copies[-1].start()
    for copy in copies:
        copy.wait()


VMEM = pl.BlockSpec(memory_space=pltpu.VMEM)
PARAMS = pltpu.CompilerParams(vmem_limit_bytes=12 * 1024 * 1024)


def call(body, name, shapes, ins):
    return pl.pallas_call(
        body,
        out_shape=shapes,
        in_specs=ins,
        out_specs=jax.tree.map(lambda _: VMEM, shapes),
        compiler_params=PARAMS,
        name=name,
    )


def on_device(acts, grads_out, act_inverse, grad_inverse):
    bf16, f32 = jnp.bfloat16, jnp.float32
    shape = jax.ShapeDtypeStruct
    c = lax.axis_index("c")
    first = c == 0

    block = jnp.stack([acts.T, grads_out.T])
    line = stacked(along_line, block, ORDER_Z)
    held = turned(first_turn, [line] * 4)
    held = [held[k] for k in ORDER_2]
    act_plane = jnp.stack([part[:, 0] for part in held])
    grad_plane = jnp.stack([part[:, 1] for part in held])

    def factor(rows):
        theirs = swap_cores(rows)
        return jnp.where(first, rows, theirs), jnp.where(first, theirs, rows)

    def partial(turns, pieces, rest, rows, flip):
        ins = [pieces[k] for k in turns] + rest + list(rows)
        return call(
            functools.partial(precondition, turns, flip),
            "precondition",
            shape((128, 128), f32),
            [VMEM] * len(ins),
        )(*ins)

    act_rows, grad_rows = factor(act_inverse), factor(grad_inverse)
    pieces = turned(second_turn, [act_plane] * 4)
    part = partial((0, 3, 1), pieces, [], act_rows, False)
    part = partial((2,), pieces, [part], act_rows, True)
    part, grad_plane = lax.optimization_barrier((part, grad_plane))
    act = (part + swap_cores(part)).astype(bf16)
    half = jnp.stack([grad_plane, second_turn(grad_plane, 1)])

    there = [to_parity(act, j, 1) for j in (0, 1)]
    here = [to_parity(act, j, 0) for j in (0, 1)]
    half, here[0] = lax.optimization_barrier((half, here[0]))
    rest = second_turn(half, 3)
    grad_pieces = half[0], half[1], rest[1], rest[0]
    pair = jnp.stack([*here, *there]).reshape(2, 2, 128, 128)
    pair = jnp.swapaxes(pair, 0, 1).reshape(2, 256, 128)
    part = partial((0, 1, 2, 3), grad_pieces, [], grad_rows, False)
    plane = stacked(first_turn, pair, ORDER_B)
    grad = (part + swap_cores(part)).astype(bf16)
    grad = jnp.where(first, grad, jnp.concatenate([grad[64:], grad[:64]], axis=0))
    grad = jnp.concatenate([grad, swap_reps(grad)], axis=1)

    made = [
        call(tile, "tile", [shape((64, 1024), f32)] * 2, [VMEM] * 2)(grad, piece)
        for piece in turned(second_turn, [plane] * 4)
    ]
    own = [made[k][0] for k in ORDER_F]
    sibling = [swap_cores(made[k][1]) for k in ORDER_F]
    return pl.pallas_call(
        assemble,
        out_shape=shape((64, 8192), f32),
        in_specs=[VMEM] * 8,
        out_specs=pl.BlockSpec(memory_space=pltpu.HBM),
        scratch_shapes=[pltpu.VMEM((64, 8192), f32), pltpu.SemaphoreType.DMA((4,))],
        compiler_params=PARAMS,
        name="assemble",
    )(*own, *sibling)


def solution(mesh):
    finer = Mesh(mesh.devices.reshape(SIZES), AXES)
    return jax.shard_map(
        on_device,
        mesh=finer,
        in_specs=(P("rep", ZERO), P("rep", ZERO), P(ZERO, None), P(ZERO, None)),
        out_specs=P(ZERO, None),
        check_vma=False,
    )
```

```python
import functools

import jax
import jax.numpy as jnp
from jax import lax
from jax.experimental import pallas as pl
from jax.experimental.pallas import tpu as pltpu
from jax.sharding import Mesh
from jax.sharding import PartitionSpec as P

AXES = ("rep", "zl", "y", "x", "c")
SIZES = (2, 4, 4, 4, 2)
ZERO = AXES[1:]
TOKENS = 256


def places():
    for r in range(2):
        for zl in range(4):
            for y in range(4):
                for x in range(4):
                    for c in range(2):
                        yield r, zl, y, x, c


def rank(r, zl, y, x, c):
    return (((r * 4 + zl) * 4 + y) * 4 + x) * 2 + c


def send(value, target):
    pairs = [(rank(*place), rank(*target(*place))) for place in places()]
    return lax.ppermute(value, AXES, pairs)


def swap_cores(value):
    return send(value, lambda r, zl, y, x, c: (r, zl, y, x, 1 - c))


def swap_reps(value):
    return send(value, lambda r, zl, y, x, c: (1 - r, zl, y, x, c))


def along_line(value, k):
    return send(value, lambda r, zl, y, x, c: (r, zl ^ k, y, x, c))


def first_turn(value, k):
    return send(
        value,
        lambda r, zl, y, x, c: (r, zl, y, x ^ k, c) if c else (r, zl, y ^ k, x, c),
    )


def second_turn(value, k):
    return send(
        value,
        lambda r, zl, y, x, c: (r, zl, y ^ k, x, c) if c else (r, zl, y, x ^ k, c),
    )


def stacked(turn, value, order):
    got = turned(turn, [value] * 4)
    return jnp.stack([got[k] for k in order])


def to_parity(value, j, other_rep):
    def target(r, zl, y, x, c):
        return r ^ other_rep, zl ^ (2 * j + c), y, x, zl % 2

    return send(value, target)


def turned(turn, values):
    got = {k: turn(values[k], k) for k in (1, 3, 2)}
    return [values[0]] + [got[k] for k in (1, 2, 3)]


ORDER_F = (0, 1, 3, 2)
ORDER_Z, ORDER_2, ORDER_B = (0, 2, 1, 3), (0, 2, 1, 3), (0, 2, 1, 3)


def here_is():
    return [lax.axis_index(name) for name in ("zl", "y", "x", "c")]


def column(where, core, k3, k2, z):
    y = where[1] ^ jnp.where(core == 0, k2, k3)
    x = where[2] ^ jnp.where(core == 0, k3, k2)
    return pl.multiple_of(((z * 4 + y) * 4 + x) * 128, 128)


def precondition(turns, flip, *refs):
    where = here_is()
    pieces, (low, high), pre = refs[: len(turns)], refs[-3:-1], refs[-1]
    rest = refs[len(turns) : -3]
    total = rest[0][...] if rest else jnp.zeros((128, 128), jnp.float32)
    none = jnp.zeros((64, 128), jnp.bfloat16)
    for k3, piece in zip(turns, pieces):
        for n, k2 in enumerate(ORDER_2):
            at = [
                pl.ds(column(where, where[3], k3, k2, where[0] ^ kz), 128)
                for kz in ORDER_Z
            ]
            rows = jnp.concatenate(
                [
                    jnp.concatenate([side[:, part] for part in at], axis=1)
                    for side in (low, high)
                ],
                axis=0,
            )
            held = []
            for m in range(4):
                block = piece[n, m]
                held.append(jnp.where(where[3] == 0, block, none))
                held.append(jnp.where(where[3] == 0, none, block))
            total += jnp.dot(
                rows,
                jnp.concatenate(held, axis=0),
                preferred_element_type=jnp.float32,
            )
    pre[...] = total.T if flip else total


def tile(g, piece, keep, give):
    blocks = [piece[k2, j] for k2 in range(4) for j in range(2)]
    part = jnp.dot(
        g[...],
        jnp.concatenate(blocks, axis=1),
        preferred_element_type=jnp.float32,
    ) * (1.0 / TOKENS)
    keep[...] = part[:64]
    give[...] = part[64:]


def assemble(*refs):
    where = here_is()
    pieces, (out, wide, sems) = refs[:8], refs[8:]
    core = where[3]
    places = []
    for side in range(2):
        held_by = core if side == 0 else 1 - core
        for m, k3 in enumerate(ORDER_F):
            for n, k2 in enumerate(ORDER_B):
                for j in range(2):
                    z = where[0] ^ (2 * j + lax.rem(where[0] + held_by, 2))
                    at = column(where, held_by, k3, k2, z)
                    places.append((pieces[side * 4 + m], (n * 2 + j) * 128, at))
    copies = []
    for i in range(4):
        rows = slice(i * 16, i * 16 + 16)
        for piece, b, at in places:
            wide[rows, pl.ds(at, 128)] = piece[rows, b : b + 128]
        copies.append(pltpu.make_async_copy(wide.at[rows], out.at[rows], sems.at[i]))
        copies[-1].start()
    for copy in copies:
        copy.wait()


VMEM = pl.BlockSpec(memory_space=pltpu.VMEM)
PARAMS = pltpu.CompilerParams(vmem_limit_bytes=12 * 1024 * 1024)


def call(body, name, shapes, ins):
    return pl.pallas_call(
        body,
        out_shape=shapes,
        in_specs=ins,
        out_specs=jax.tree.map(lambda _: VMEM, shapes),
        compiler_params=PARAMS,
        name=name,
    )


def on_device(acts, grads_out, act_inverse, grad_inverse):
    bf16, f32 = jnp.bfloat16, jnp.float32
    shape = jax.ShapeDtypeStruct
    c = lax.axis_index("c")
    first = c == 0

    block = jnp.stack([acts.T, grads_out.T])
    line = stacked(along_line, block, ORDER_Z)
    held = turned(first_turn, [line] * 4)
    held = [held[k] for k in ORDER_2]
    act_plane = jnp.stack([part[:, 0] for part in held])
    grad_plane = jnp.stack([part[:, 1] for part in held])

    def factor(rows):
        theirs = swap_cores(rows)
        return jnp.where(first, rows, theirs), jnp.where(first, theirs, rows)

    def partial(turns, pieces, rest, rows, flip):
        ins = [pieces[k] for k in turns] + rest + list(rows)
        return call(
            functools.partial(precondition, turns, flip),
            "precondition",
            shape((128, 128), f32),
            [VMEM] * len(ins),
        )(*ins)

    act_rows, grad_rows = factor(act_inverse), factor(grad_inverse)
    pieces = turned(second_turn, [act_plane] * 4)
    part = partial((0, 2, 3), pieces, [], act_rows, False)
    part = partial((1,), pieces, [part], act_rows, True)
    part, grad_plane = lax.optimization_barrier((part, grad_plane))
    act = (part + swap_cores(part)).astype(bf16)
    half = jnp.stack([grad_plane, second_turn(grad_plane, 1)])

    there = [to_parity(act, j, 1) for j in (0, 1)]
    here = [to_parity(act, j, 0) for j in (0, 1)]
    half, here[0] = lax.optimization_barrier((half, here[0]))
    rest = second_turn(half, 3)
    pair = jnp.stack([*there, *here]).reshape(2, 2, 128, 128)
    pair = jnp.swapaxes(pair, 0, 1).reshape(2, 256, 128)
    plane = stacked(first_turn, pair, ORDER_B)
    plane, rest = lax.optimization_barrier((plane, rest))
    grad_pieces = half[0], half[1], rest[1], rest[0]
    part = partial((0, 1, 2, 3), grad_pieces, [], grad_rows, False)
    grad = (part + swap_cores(part)).astype(bf16)
    grad = jnp.where(first, grad, jnp.concatenate([grad[64:], grad[:64]], axis=0))
    grad = jnp.concatenate([swap_reps(grad), grad], axis=1)

    made = [
        call(tile, "tile", [shape((64, 1024), f32)] * 2, [VMEM] * 2)(grad, piece)
        for piece in turned(second_turn, [plane] * 4)
    ]
    own = [made[k][0] for k in ORDER_F]
    sibling = [swap_cores(made[k][1]) for k in ORDER_F]
    return pl.pallas_call(
        assemble,
        out_shape=shape((64, 8192), f32),
        in_specs=[VMEM] * 8,
        out_specs=pl.BlockSpec(memory_space=pltpu.HBM),
        scratch_shapes=[pltpu.VMEM((64, 8192), f32), pltpu.SemaphoreType.DMA((4,))],
        compiler_params=PARAMS,
        name="assemble",
    )(*own, *sibling)


def solution(mesh):
    finer = Mesh(mesh.devices.reshape(SIZES), AXES)
    return jax.shard_map(
        on_device,
        mesh=finer,
        in_specs=(P("rep", ZERO), P("rep", ZERO), P(ZERO, None), P(ZERO, None)),
        out_specs=P(ZERO, None),
        check_vma=False,
    )
```

```python
import functools

import jax
import jax.numpy as jnp
from jax import lax
from jax.experimental import pallas as pl
from jax.experimental.pallas import tpu as pltpu
from jax.sharding import Mesh
from jax.sharding import PartitionSpec as P

AXES = ("rep", "zl", "y", "x", "c")
SIZES = (2, 4, 4, 4, 2)
ZERO = AXES[1:]
TOKENS = 256


def places():
    for r in range(2):
        for zl in range(4):
            for y in range(4):
                for x in range(4):
                    for c in range(2):
                        yield r, zl, y, x, c


def rank(r, zl, y, x, c):
    return (((r * 4 + zl) * 4 + y) * 4 + x) * 2 + c


def send(value, target):
    pairs = [(rank(*place), rank(*target(*place))) for place in places()]
    return lax.ppermute(value, AXES, pairs)


def swap_cores(value):
    return send(value, lambda r, zl, y, x, c: (r, zl, y, x, 1 - c))


def swap_reps(value):
    return send(value, lambda r, zl, y, x, c: (1 - r, zl, y, x, c))


def along_line(value, k):
    return send(value, lambda r, zl, y, x, c: (r, zl ^ k, y, x, c))


def first_turn(value, k):
    return send(
        value,
        lambda r, zl, y, x, c: (r, zl, y, x ^ k, c) if c else (r, zl, y ^ k, x, c),
    )


def second_turn(value, k):
    return send(
        value,
        lambda r, zl, y, x, c: (r, zl, y ^ k, x, c) if c else (r, zl, y, x ^ k, c),
    )


def stacked(turn, value, order):
    got = turned(turn, [value] * 4)
    return jnp.stack([got[k] for k in order])


def to_parity(value, j, other_rep):
    def target(r, zl, y, x, c):
        return r ^ other_rep, zl ^ (2 * j + c), y, x, zl % 2

    return send(value, target)


def turned(turn, values):
    got = {k: turn(values[k], k) for k in (1, 3, 2)}
    return [values[0]] + [got[k] for k in (1, 2, 3)]


ORDER_F = (0, 2, 1, 3)
ORDER_Z, ORDER_2, ORDER_B = (0, 1, 2, 3), (0, 1, 3, 2), (0, 1, 3, 2)


def here_is():
    return [lax.axis_index(name) for name in ("zl", "y", "x", "c")]


def column(where, core, k3, k2, z):
    y = where[1] ^ jnp.where(core == 0, k2, k3)
    x = where[2] ^ jnp.where(core == 0, k3, k2)
    return pl.multiple_of(((z * 4 + y) * 4 + x) * 128, 128)


def precondition(turns, flip, *refs):
    where = here_is()
    pieces, (low, high), pre = refs[: len(turns)], refs[-3:-1], refs[-1]
    rest = refs[len(turns) : -3]
    total = rest[0][...] if rest else jnp.zeros((128, 128), jnp.float32)
    none = jnp.zeros((64, 128), jnp.bfloat16)
    for k3, piece in zip(turns, pieces):
        for n, k2 in enumerate(ORDER_2):
            at = [
                pl.ds(column(where, where[3], k3, k2, where[0] ^ kz), 128)
                for kz in ORDER_Z
            ]
            rows = jnp.concatenate(
                [
                    jnp.concatenate([side[:, part] for part in at], axis=1)
                    for side in (low, high)
                ],
                axis=0,
            )
            held = []
            for m in range(4):
                block = piece[n, m]
                held.append(jnp.where(where[3] == 0, block, none))
                held.append(jnp.where(where[3] == 0, none, block))
            total += jnp.dot(
                rows,
                jnp.concatenate(held, axis=0),
                preferred_element_type=jnp.float32,
            )
    pre[...] = total.T if flip else total


def tile(g, piece, keep, give):
    blocks = [piece[k2, j] for k2 in range(4) for j in range(2)]
    part = jnp.dot(
        g[...],
        jnp.concatenate(blocks, axis=1),
        preferred_element_type=jnp.float32,
    ) * (1.0 / TOKENS)
    keep[...] = part[:64]
    give[...] = part[64:]


def assemble(*refs):
    where = here_is()
    pieces, (out, wide, sems) = refs[:8], refs[8:]
    core = where[3]
    places = []
    for side in range(2):
        held_by = core if side == 0 else 1 - core
        for m, k3 in enumerate(ORDER_F):
            for n, k2 in enumerate(ORDER_B):
                for j in range(2):
                    z = where[0] ^ (2 * j + lax.rem(where[0] + held_by, 2))
                    at = column(where, held_by, k3, k2, z)
                    places.append((pieces[side * 4 + m], (n * 2 + j) * 128, at))
    copies = []
    for i in range(4):
        rows = slice(i * 16, i * 16 + 16)
        for piece, b, at in places:
            wide[rows, pl.ds(at, 128)] = piece[rows, b : b + 128]
        copies.append(pltpu.make_async_copy(wide.at[rows], out.at[rows], sems.at[i]))
        copies[-1].start()
    for copy in copies:
        copy.wait()


VMEM = pl.BlockSpec(memory_space=pltpu.VMEM)
PARAMS = pltpu.CompilerParams(vmem_limit_bytes=12 * 1024 * 1024)


def call(body, name, shapes, ins):
    return pl.pallas_call(
        body,
        out_shape=shapes,
        in_specs=ins,
        out_specs=jax.tree.map(lambda _: VMEM, shapes),
        compiler_params=PARAMS,
        name=name,
    )


def on_device(acts, grads_out, act_inverse, grad_inverse):
    bf16, f32 = jnp.bfloat16, jnp.float32
    shape = jax.ShapeDtypeStruct
    c = lax.axis_index("c")
    first = c == 0

    block = jnp.stack([acts.T, grads_out.T])
    line = stacked(along_line, block, ORDER_Z)
    held = turned(first_turn, [line] * 4)
    held = [held[k] for k in ORDER_2]
    act_plane = jnp.stack([part[:, 0] for part in held])
    grad_plane = jnp.stack([part[:, 1] for part in held])

    def factor(rows):
        theirs = swap_cores(rows)
        return jnp.where(first, rows, theirs), jnp.where(first, theirs, rows)

    def partial(turns, pieces, rest, rows, flip):
        ins = [pieces[k] for k in turns] + rest + list(rows)
        return call(
            functools.partial(precondition, turns, flip),
            "precondition",
            shape((128, 128), f32),
            [VMEM] * len(ins),
        )(*ins)

    act_rows, grad_rows = factor(act_inverse), factor(grad_inverse)
    pieces = turned(second_turn, [act_plane] * 4)
    part = partial((0, 3, 1), pieces, [], act_rows, False)
    part = partial((2,), pieces, [part], act_rows, True)
    part, grad_plane = lax.optimization_barrier((part, grad_plane))
    act = (part + swap_cores(part)).astype(bf16)
    half = jnp.stack([grad_plane, second_turn(grad_plane, 1)])

    there = [to_parity(act, j, 1) for j in (0, 1)]
    here = [to_parity(act, j, 0) for j in (0, 1)]
    rest = second_turn(half, 3)
    grad_pieces = half[0], half[1], rest[1], rest[0]
    pair = jnp.stack([*here, *there]).reshape(2, 2, 128, 128)
    pair = jnp.swapaxes(pair, 0, 1).reshape(2, 256, 128)
    part = partial((0, 1, 2, 3), grad_pieces, [], grad_rows, False)
    plane = stacked(first_turn, pair, ORDER_B)
    grad = (part + swap_cores(part)).astype(bf16)
    grad = jnp.where(first, grad, jnp.concatenate([grad[64:], grad[:64]], axis=0))
    grad = jnp.concatenate([grad, swap_reps(grad)], axis=1)

    made = [
        call(tile, "tile", [shape((64, 1024), f32)] * 2, [VMEM] * 2)(grad, piece)
        for piece in turned(second_turn, [plane] * 4)
    ]
    own = [made[k][0] for k in ORDER_F]
    sibling = [swap_cores(made[k][1]) for k in ORDER_F]
    return pl.pallas_call(
        assemble,
        out_shape=shape((64, 8192), f32),
        in_specs=[VMEM] * 8,
        out_specs=pl.BlockSpec(memory_space=pltpu.HBM),
        scratch_shapes=[pltpu.VMEM((64, 8192), f32), pltpu.SemaphoreType.DMA((4,))],
        compiler_params=PARAMS,
        name="assemble",
    )(*own, *sibling)


def solution(mesh):
    finer = Mesh(mesh.devices.reshape(SIZES), AXES)
    return jax.shard_map(
        on_device,
        mesh=finer,
        in_specs=(P("rep", ZERO), P("rep", ZERO), P(ZERO, None), P(ZERO, None)),
        out_specs=P(ZERO, None),
        check_vma=False,
    )
```
